128 devices in a mesh: mem: 2 (over core), state: 64 (over y, x, z).
Axes of the slice: x: 4, y: 4, z: 4, core: 2. Of those that a mesh axis runs over, the one named last changes fastest.
Arguments:
- background_ensemble: bfloat16 [80, 4194304], P('mem', 'state'), may hold values from -6 to 6
- measured_segment_index: int32 [2, 256], replicated, may hold values from 0 to 127
- measured_place_within_segment: int32 [2, 256], replicated, may hold values from 0 to 32767
- measured_readings: float32 [2, 256], replicated, may hold values from -6 to 6
- measured_noise_spread: float32 [2, 256], replicated, may hold values from 0.25 to 4
- measured_damping_weight: float32 [2, 256], replicated, may hold values from 0.3 to 1
- measured_cutoff_extent: int32 [2, 256], replicated, may hold values from 1 to 1024
Outputs:
- analysis: bfloat16 [80, 4194304], P('mem', 'state')
The draws below stay inside these ranges and needn't reach their ends.
Inputs may be any that keep to these rules, and one draw needn't show every extreme that they name: measured_segment_index numbers the blocks of 32768 state values in the order of the state dimension. measured_place_within_segment is a position inside the owner's block.
All inputs are finite; a program needn't handle non-finite values.
Results may differ from the reference program's by a relative error of at most 0.0051.
Values may be sent and summed in bfloat16 or wider, within the bound.
No kernel may reach another device: no remote copies, remote signals or barrier semaphores. Data moves between devices by JAX's collectives and lax.ppermute only.
A program may use at most 64 MiB of HBM per device.

```python
import math
import jax
import jax.numpy as jnp
import numpy as np
from jax import lax

ENSEMBLE_COUNT = 80
SD = 32768
K = 256
B = 2
LB = 128
BLK = 4096
GRID_UNKNOWNS = 4194304
N_MEM = 2
N_STATE = 64


def place_ends(drawn, rng, low, high):
    extent = drawn.shape
    index_at = [jax.random.randint(jax.random.fold_in(rng, axis), (), 0, extent[axis]) for axis in range(len(extent))]
    drawn = drawn.at[tuple(index_at)].set(low)
    longest = extent.index(max(extent))
    index_at[longest] = (index_at[longest] + 1) % extent[longest]
    return drawn.at[tuple(index_at)].set(high)


def block_levels(stream_key, shape, split, low, top_value):
    def one(axis_at, blocks):
        draws = jax.random.uniform(jax.random.fold_in(jax.random.fold_in(stream_key, 6), axis_at), (blocks,), jnp.float32, low / len(split), top_value / len(split))
        return jnp.repeat(jnp.exp(draws), shape[axis_at] // blocks).reshape((-1,) + (1,) * (len(shape) - axis_at - 1))

    loudness = one(*split[0])
    for cut in split[1:]:
        loudness = loudness * one(*cut)
    return loudness


def cumulative_ranks(count, skew):
    weights = [(1 << 20) // math.isqrt(standing ** skew) + 1 for standing in range(1, count + 1)]
    spread = 1 + sum(weights) // (1 << 30)
    return np.cumsum(np.array([max(1, weight // spread) for weight in weights]))


def ranked_ids(stream_key, extent, number_of, slope):
    grid = cumulative_ranks(number_of, slope)
    lot = jax.random.randint(jax.random.fold_in(stream_key, 1), extent, 0, int(grid[number_of - 1]))
    standing = jnp.searchsorted(jnp.asarray(grid, jnp.int32), lot, side="right")
    return jax.random.permutation(jax.random.fold_in(stream_key, 2), number_of)[standing].astype(jnp.int32)


def normal_values(own_key, extent, scale, reach, cuts=(), held_as=jnp.bfloat16):
    result = jax.random.normal(own_key, extent, jnp.float32) * scale
    if len(cuts) > 0:
        result = block_levels(own_key, extent, cuts, -0.22, 0.18) * result
    return jnp.clip(result, min=-reach, max=reach).astype(held_as)


def setup_inputs(seed: int = 0) -> dict:
    seeds = jax.random.split(jax.random.key(seed), 8)
    return {
        "background_ensemble": normal_values(seeds[0], (ENSEMBLE_COUNT, GRID_UNKNOWNS), 1.0, 6.0, ((0, 2), (1, 64))),
        "measured_segment_index": place_ends(ranked_ids(seeds[1], (B, K), N_MEM * N_STATE, 2), jax.random.fold_in(seeds[1], 3), 0, (N_MEM * N_STATE) - 1).astype(jnp.int32),
        "measured_place_within_segment": place_ends(jax.random.randint(seeds[2], (B, K), 0, SD), jax.random.fold_in(seeds[2], 1), 0, SD - 1).astype(jnp.int32),
        "measured_readings": normal_values(seeds[3], (B, K), 1.5, 6.0, (), jnp.float32),
        "measured_noise_spread": jnp.clip(jnp.exp(jax.random.uniform(seeds[4], (B, K), jnp.float32, math.log(0.25), math.log(4.0))), 0.25, 4.0),
        "measured_damping_weight": jnp.clip(jax.random.uniform(seeds[5], (B, K), jnp.float32, 0.3, 1.0), 0.3, 1.0),
        "measured_cutoff_extent": place_ends(jax.random.randint(seeds[6], (B, K), 1, 4 * SD // LB + 1), jax.random.fold_in(seeds[6], 1), 1, (4 * SD // LB + 1) - 1).astype(jnp.int32),
    }


def observe_stats(prior_ens, values, variances):
    centre = lax.optimization_barrier(jnp.mean(prior_ens, axis=0))
    anomaly = prior_ens - centre
    prior_var = lax.optimization_barrier(jnp.sum(anomaly * anomaly, axis=0)) / (ENSEMBLE_COUNT - 1) + 1e-06
    post_var = 1.0 / (1.0 / prior_var + 1.0 / variances)
    post_mean = post_var * (centre / prior_var + values / variances)
    shrink = jnp.sqrt(post_var / prior_var)
    increment = (post_mean - centre + (shrink - 1.0) * anomaly).astype(jnp.bfloat16)
    scaling = 1.0 / ((ENSEMBLE_COUNT - 1) * prior_var)
    return (increment, anomaly.astype(jnp.bfloat16), scaling)

def taper_weights(columns, obs_index, taper_row, reach_row):
    distance = jnp.abs(columns[:, None] // LB - obs_index[None, :] // LB).astype(jnp.float32)
    return taper_row[None, :] * jnp.maximum(0.0, 1.0 - distance / (reach_row[None, :].astype(jnp.float32) + 1.0))

def update_block(block_values, columns, obs_index, taper_row, reach_row, increment, anomaly, scaling):
    values = block_values.astype(jnp.float32)
    centred = (values - lax.optimization_barrier(jnp.mean(values, axis=0))).astype(jnp.bfloat16)
    covariance = lax.dot_general(centred, anomaly, (((0,), (0,)), ((), ())), preferred_element_type=jnp.float32)
    gain_matrix = (taper_weights(columns, obs_index, taper_row, reach_row) * covariance * scaling[None, :]).astype(jnp.bfloat16)
    change = lax.dot_general(increment, gain_matrix, (((1,), (1,)), ((), ())), preferred_element_type=jnp.float32)
    return (values + change).astype(jnp.bfloat16)

def reference(background_ensemble, measured_segment_index, measured_place_within_segment, measured_readings, measured_noise_spread, measured_damping_weight, measured_cutoff_extent):
    realization_vectors = background_ensemble
    total_cols = realization_vectors.shape[1]
    for batch_no in range(B):
        obs_index = (measured_segment_index[batch_no] * SD + measured_place_within_segment[batch_no]).astype(jnp.int32)
        prior_ens = jnp.take(realization_vectors, obs_index, axis=1).astype(jnp.float32)
        increment, anomaly, scaling = observe_stats(prior_ens, measured_readings[batch_no], measured_noise_spread[batch_no])
        current = realization_vectors
        taper_row = measured_damping_weight[batch_no]
        reach_row = measured_cutoff_extent[batch_no]

        def per_block(block_no):
            start_col = (block_no * BLK).astype(jnp.int32)
            block_values = lax.dynamic_slice_in_dim(current, start_col, BLK, 1)
            columns = start_col + jnp.arange(BLK, dtype=jnp.int32)
            return update_block(block_values, columns, obs_index, taper_row, reach_row, increment, anomaly, scaling)
        updated = lax.map(per_block, jnp.arange(total_cols // BLK, dtype=jnp.int32))
        realization_vectors = jnp.transpose(updated, (1, 0, 2)).reshape(realization_vectors.shape[0], total_cols)
    return realization_vectors
```

```python
import functools

import jax
import jax.numpy as jnp
from jax import lax
from jax.experimental import pallas as pl
from jax.experimental.pallas import tpu as pltpu
from jax.sharding import PartitionSpec as P

MEMBERS = 80
HALF = 40
SD = 32768
K = 256
B = 2
LB = 128
CHIP = 2 * SD
CHIPS = 64
SEG_BLOCKS = SD // LB
CHUNK = 2048
STEPS = SD // CHUNK
CHUNK_BLOCKS = CHUNK // LB
F32 = jnp.float32
BF16 = jnp.bfloat16
NT = (((1,), (1,)), ((), ()))
VMEM_LIMIT = 56 * 1024 * 1024


def dot(a, b):
    return jnp.dot(a, b, preferred_element_type=F32)


def dot_nt(a, b):
    return lax.dot_general(a, b, NT, preferred_element_type=F32)


def pick_kernel(rel_ref, x_ref, o_ref, xv, acc, owned, sems):
    parts = 4
    width = CHIP // parts
    copies = [
        pltpu.make_async_copy(
            x_ref.at[:, pl.ds(p * width, width)], xv.at[:, pl.ds(p * width, width)], sems.at[p]
        )
        for p in range(parts)
    ]
    for copy in copies:
        copy.start()
    acc[...] = jnp.zeros_like(acc)

    def scan(k, n):
        owned[n] = k
        return n + (rel_ref[k] >= 0).astype(jnp.int32)

    n = lax.fori_loop(0, B * K, scan, jnp.int32(0), unroll=8)
    for j in range(4):
        owned[n + j] = B * K
    for copy in copies:
        copy.wait()
    lane = lax.broadcasted_iota(jnp.int32, (HALF, LB), 1)

    def extract(i, _):
        for j in range(4):
            k = owned[4 * i + j]
            at = rel_ref[k]
            start = pl.multiple_of((at // LB) * LB, LB)
            tile = xv[:, pl.ds(start, LB)].astype(F32)
            turned = pltpu.roll(tile, (k - at) & (LB - 1), 1)
            pltpu.store(acc.at[k // LB], turned, mask=lane == (k & (LB - 1)))
        return 0

    lax.fori_loop(0, (n + 3) // 4, extract, 0)
    for g in range(B * K // LB):
        o_ref[:, g * LB : (g + 1) * LB] = acc[g].astype(BF16)


def pick(rel, x):
    return pl.pallas_call(
        pick_kernel,
        grid_spec=pltpu.PrefetchScalarGridSpec(
            num_scalar_prefetch=1,
            grid=(1,),
            in_specs=[pl.BlockSpec(memory_space=pl.ANY)],
            out_specs=pl.BlockSpec((HALF, B * K), lambda i, s: (0, 0)),
            scratch_shapes=[
                pltpu.VMEM((HALF, CHIP), BF16),
                pltpu.VMEM((B * K // LB + 1, HALF, LB), F32),
                pltpu.SMEM((B * K + 8,), jnp.int32),
                pltpu.SemaphoreType.DMA((4,)),
            ],
        ),
        out_shape=jax.ShapeDtypeStruct((HALF, B * K), BF16),
        compiler_params=pltpu.CompilerParams(vmem_limit_bytes=VMEM_LIMIT),
        cost_estimate=pl.CostEstimate(flops=0, bytes_accessed=2 * HALF * CHIP, transcendentals=0),
        name="pick",
    )(rel, x)


def observe_stats(prior, values, variances):
    centre = jnp.sum(prior, axis=0, keepdims=True) / MEMBERS
    anomaly = prior - centre
    prior_var = jnp.sum(anomaly * anomaly, axis=0, keepdims=True) / (MEMBERS - 1) + 1e-06
    post_var = 1.0 / (1.0 / prior_var + 1.0 / variances)
    post_mean = post_var * (centre / prior_var + values / variances)
    shrink = jnp.sqrt(post_var / prior_var)
    increment = (post_mean - centre + (shrink - 1.0) * anomaly).astype(BF16)
    scaled = anomaly * (1.0 / ((MEMBERS - 1) * prior_var))
    high = scaled.astype(BF16)
    low = (scaled - high.astype(F32)).astype(BF16)
    return increment, high, low


def iota(shape, dim):
    return lax.broadcasted_iota(jnp.int32, shape, dim)


def update_kernel(
    sp_ref, row_ref, col_ref, prior_ref, x_ref, own_ref, away_ref, cov_l, chg_l, cols, count
):
    step = pl.program_id(0)
    first = sp_ref[1].astype(F32)

    @pl.when(step == 0)
    def _():
        row = lambda r: row_ref[r : r + 1, :]
        eye = (iota((K, K), 0) == iota((K, K), 1)).astype(F32).astype(BF16)
        upper = (iota((K, K), 0) <= iota((K, K), 1)).astype(F32).astype(BF16)
        member_eye = (iota((MEMBERS, LB), 0) == iota((MEMBERS, LB), 1)).astype(F32).astype(BF16)
        prior0 = prior_ref[:, :K].astype(F32)
        stats0 = observe_stats(prior0, row(6), row(8))
        prior1b = prior_ref[:, K:]
        lhs = jnp.concatenate([dot_nt(eye, stats0[1]), dot_nt(eye, stats0[2])], 1).astype(BF16)
        cov = dot(lhs, jnp.concatenate([prior1b, prior1b], 0))
        distance = jnp.abs(row(1) - col_ref[:, 0:1])
        weight = col_ref[:, 2:3] * jnp.maximum(0.0, 1.0 - distance / col_ref[:, 1:2])
        gain = (weight * cov).astype(BF16)
        prior1 = (prior1b.astype(F32) + dot(stats0[0], gain)).astype(BF16).astype(F32)
        stats1 = observe_stats(prior1, row(7), row(9))
        most = jnp.int32(0)
        for b, (increment, high, low) in enumerate((stats0, stats1)):
            place, reach, damping = row(b), row(2 + b), row(4 + b)
            last = first + (SEG_BLOCKS - 1)
            gap = jnp.maximum(jnp.maximum(first - place, place - last), 0.0)
            felt = (gap < reach).astype(F32)
            rank = dot(jnp.broadcast_to(felt, (8, K)).astype(BF16), upper)[0:1]
            slot = jnp.where(felt > 0.0, rank - 1.0, -1.0)
            chosen = slot == iota((K, K), 0).astype(F32)
            most = jnp.maximum(most, jnp.sum(felt).astype(jnp.int32))
            pickm = chosen.astype(F32).astype(BF16)
            cov_l[b] = jnp.concatenate([dot_nt(pickm, high), dot_nt(pickm, low)], 1).astype(BF16)
            chg_l[b, :, 0:K] = dot_nt(increment, pickm).astype(BF16)
            chg_l[b, :, K : K + LB] = member_eye
            for c, value in enumerate((place, reach, damping)):
                column = jnp.sum(jnp.where(chosen, value, 0.0), axis=1, keepdims=True)
                if c == 1:
                    column = jnp.maximum(column, 1.0)
                cols[b, c] = jnp.broadcast_to(column, (K, LB))
        count[0] = most

    def weights(b, kc):
        block = (first + (step * CHUNK_BLOCKS).astype(F32)) + iota((kc, LB), 1).astype(F32)
        distance = jnp.abs(block - cols[b, 0, :kc])
        return cols[b, 2, :kc] * jnp.maximum(0.0, 1.0 - distance / cols[b, 1, :kc])

    def gains(b, kc, x, w, pair):
        cov = dot(cov_l[b, :kc], jnp.concatenate([x, x], 0))
        parts = [
            cov[:, h * LB : (h + 1) * LB]
            * jnp.broadcast_to(w[:, 2 * pair + h : 2 * pair + h + 1], (kc, LB))
            for h in range(2)
        ]
        return jnp.concatenate(parts, 1).astype(BF16)

    def advance(kc):
        w = [weights(b, kc) for b in range(B)]
        for pair in range(CHUNK // 256):
            x = x_ref[:, pair * 256 : (pair + 1) * 256]
            for b in range(B):
                g = gains(b, kc, x, w[b], pair)
                if kc == LB:
                    lhs = jnp.concatenate([chg_l[b, :, 0:LB], chg_l[b, :, K : K + LB]], 1)
                    spare = jnp.zeros((LB - MEMBERS, 256), BF16)
                    after = dot(lhs, jnp.concatenate([g, x, spare], 0))
                else:
                    after = dot(chg_l[b, :, 0:K], g) + x.astype(F32)
                if b == 0:
                    x = after.astype(BF16)
            own_ref[:, pair * 256 : (pair + 1) * 256] = after[:HALF].astype(BF16)
            away_ref[:, pair * 256 : (pair + 1) * 256] = after[HALF:].astype(BF16)

    @pl.when(count[0] <= LB)
    def _():
        advance(LB)

    @pl.when(count[0] > LB)
    def _():
        advance(K)


def update(sp, rows, cols, prior, x):
    return pl.pallas_call(
        update_kernel,
        grid_spec=pltpu.PrefetchScalarGridSpec(
            num_scalar_prefetch=1,
            grid=(STEPS,),
            in_specs=[
                pl.BlockSpec((16, K), lambda i, s: (0, 0)),
                pl.BlockSpec((K, 8), lambda i, s: (0, 0)),
                pl.BlockSpec((MEMBERS, B * K), lambda i, s: (0, 0)),
                pl.BlockSpec((MEMBERS, CHUNK), lambda i, s: (0, i)),
            ],
            out_specs=[
                pl.BlockSpec((HALF, CHUNK), lambda i, s: (0, s[0] * STEPS + i)),
                pl.BlockSpec((HALF, CHUNK), lambda i, s: (0, i)),
            ],
            scratch_shapes=[
                pltpu.VMEM((B, K, 2 * MEMBERS), BF16),
                pltpu.VMEM((B, MEMBERS, K + LB), BF16),
                pltpu.VMEM((B, 3, K, LB), F32),
                pltpu.SMEM((1,), jnp.int32),
            ],
        ),
        out_shape=[
            jax.ShapeDtypeStruct((HALF, CHIP), BF16),
            jax.ShapeDtypeStruct((HALF, SD), BF16),
        ],
        compiler_params=pltpu.CompilerParams(vmem_limit_bytes=VMEM_LIMIT),
        cost_estimate=pl.CostEstimate(
            flops=10_000_000_000, bytes_accessed=4 * MEMBERS * SD, transcendentals=0
        ),
        name="update",
    )(sp, rows, cols, prior, x)


def fill_kernel(sp_ref, got_ref, out_hbm, out_ref):
    out_ref[...] = got_ref[...]


def fill(sp, got, out):
    width = 8192
    return pl.pallas_call(
        fill_kernel,
        grid_spec=pltpu.PrefetchScalarGridSpec(
            num_scalar_prefetch=1,
            grid=(SD // width,),
            in_specs=[
                pl.BlockSpec((HALF, width), lambda i, s: (0, i)),
                pl.BlockSpec(memory_space=pl.ANY),
            ],
            out_specs=pl.BlockSpec((HALF, width), lambda i, s: (0, (1 - s[0]) * (SD // width) + i)),
        ),
        out_shape=jax.ShapeDtypeStruct((HALF, CHIP), BF16),
        input_output_aliases={2: 0},
        compiler_params=pltpu.CompilerParams(vmem_limit_bytes=VMEM_LIMIT),
        name="fill",
    )(sp, got, out)


def shifted(array, by):
    pairs = [(i, (i + by) % CHIPS) for i in range(CHIPS)]
    return lax.ppermute(array, "state", pairs)


def swapped(array):
    return lax.ppermute(array, "mem", [(0, 1), (1, 0)])


def on_device(x, segment, place, readings, spread, damping, extent):
    core = lax.axis_index("mem")
    chip = lax.axis_index("state")
    index = segment * SD + place
    rel = index.reshape(-1) - chip * CHIP
    rel = jnp.where((rel >= 0) & (rel < CHIP), rel, -1)
    rel = jnp.concatenate([rel, jnp.zeros((8,), jnp.int32)])
    block = (index // LB).astype(F32)
    reach = extent.astype(F32) + 1.0
    rows = jnp.concatenate([block, reach, damping, readings, spread, jnp.zeros((6, K), F32)], 0)
    cols = jnp.concatenate(
        [block[0][:, None], reach[0][:, None], damping[0][:, None], jnp.zeros((K, 5), F32)], 1
    )
    sp = jnp.stack([core, (chip * 2 + core) * SEG_BLOCKS]).astype(jnp.int32)

    picked = pick(rel, x)
    sent = lax.dynamic_slice_in_dim(x, (1 - core) * SD, SD, 1)
    kept = lax.dynamic_slice_in_dim(x, core * SD, SD, 1)
    whole = jnp.concatenate([kept, swapped(sent)], 0)
    near = picked + shifted(picked, 1) + shifted(picked, -1)
    far = near + shifted(near, 3) + shifted(near, -3)
    prior = jnp.concatenate([far, swapped(far)], 0)
    own, away = update(sp, rows, cols, prior, whole)
    return fill(sp, swapped(away), own)


def solution(mesh):
    in_specs = (P("mem", "state"), P(), P(), P(), P(), P(), P())
    return jax.shard_map(
        on_device, mesh=mesh, in_specs=in_specs, out_specs=P("mem", "state"), check_vma=False
    )
```

```python
import jax
import jax.numpy as jnp
from jax import lax
from jax.experimental import pallas as pl
from jax.experimental.pallas import tpu as pltpu
from jax.sharding import PartitionSpec as P

MEMBERS = 80
HALF = 40
SD = 32768
K = 256
B = 2
LB = 128
CHIP = 2 * SD
CHIPS = 64
SEG_BLOCKS = SD // LB
CHUNK = 2048
STEPS = SD // CHUNK
CHUNK_BLOCKS = CHUNK // LB
PARTS = (7, 6, 3)
GROUP = 4
EXTRA = 16
DEPTH = MEMBERS + EXTRA
F32 = jnp.float32
BF16 = jnp.bfloat16
I32 = jnp.int32
NT = (((1,), (1,)), ((), ()))
VMEM_LIMIT = 40 * 1024 * 1024


def dot(a, b):
    return jnp.dot(a, b, preferred_element_type=F32)


def dot_nt(a, b):
    return lax.dot_general(a, b, NT, preferred_element_type=F32)


def iota(shape, dim):
    return lax.broadcasted_iota(I32, shape, dim)


def ones_where(mask):
    return mask.astype(F32).astype(BF16)


def whole(shape):
    return pl.BlockSpec(shape, lambda i, *s: (0,) * len(shape))


def pick_kernel(sp_ref, seg_ref, place_ref, x_ref, o_ref, xv, acc, owned, sems):
    parts = 4
    width = CHIP // parts
    copies = [
        pltpu.make_async_copy(
            x_ref.at[:, pl.ds(p * width, width)], xv.at[:, pl.ds(p * width, width)], sems.at[p]
        )
        for p in range(parts)
    ]
    for copy in copies:
        copy.start()
    acc[...] = jnp.zeros_like(acc)
    chip = sp_ref[2]
    n = I32(0)
    for b in range(B):

        def scan(k, n, b=b):
            owned[n] = b * K + k
            return n + ((seg_ref[b, k] >> 1) == chip).astype(I32)

        n = lax.fori_loop(0, K, scan, n, unroll=16)
    for j in range(4):
        owned[n + j] = B * K
    for copy in copies:
        copy.wait()
    lane = iota((HALF, LB), 1)

    def extract(i, _):
        for j in range(4):
            k = owned[4 * i + j]
            b = jnp.minimum(k >> 8, B - 1)
            within = k & (K - 1)
            at = (seg_ref[b, within] & 1) * SD + place_ref[b, within]
            start = pl.multiple_of((at >> 7) * LB, LB)
            tile = xv[:, pl.ds(start, LB)].astype(F32)
            turned = pltpu.roll(tile, (k - at) & (LB - 1), 1)
            pltpu.store(acc.at[k >> 7], turned, mask=lane == (k & (LB - 1)))
        return 0

    lax.fori_loop(0, (n + 3) >> 2, extract, 0)
    for g in range(B * K // LB):
        o_ref[:, g * LB : (g + 1) * LB] = acc[g].astype(BF16)


def pick(sp, segment, place, x):
    return pl.pallas_call(
        pick_kernel,
        grid_spec=pltpu.PrefetchScalarGridSpec(
            num_scalar_prefetch=3,
            grid=(1,),
            in_specs=[pl.BlockSpec(memory_space=pl.ANY)],
            out_specs=whole((HALF, B * K)),
            scratch_shapes=[
                pltpu.VMEM((HALF, CHIP), BF16),
                pltpu.VMEM((B * K // LB + 1, HALF, LB), F32),
                pltpu.SMEM((B * K + 8,), I32),
                pltpu.SemaphoreType.DMA((4,)),
            ],
        ),
        out_shape=jax.ShapeDtypeStruct((HALF, B * K), BF16),
        compiler_params=pltpu.CompilerParams(vmem_limit_bytes=VMEM_LIMIT),
        cost_estimate=pl.CostEstimate(flops=0, bytes_accessed=2 * HALF * CHIP, transcendentals=0),
        name="pick",
    )(sp, segment, place, x)


def places_kernel(
    sp_ref, seg_ref, place_ref, damp_ref, ext_ref, pick_ref, cols_ref, w_ref, count_ref
):
    first = sp_ref[1].astype(F32)
    last = first + (SEG_BLOCKS - 1)
    blocks = (seg_ref[...] * SEG_BLOCKS + (place_ref[...] >> 7)).astype(F32)
    reaches = ext_ref[...].astype(F32) + 1.0
    diagonal = iota((K, K), 0) == iota((K, K), 1)
    upper = ones_where(iota((K, K), 0) <= iota((K, K), 1))
    slots = iota((K, K), 0).astype(F32)
    most = I32(0)

    def column(mask, row):
        return jnp.sum(jnp.where(mask, row, 0.0), axis=1, keepdims=True)

    for b in range(B):
        block, reach, damping = blocks[b : b + 1], reaches[b : b + 1], damp_ref[b : b + 1, :]
        gap = jnp.maximum(jnp.maximum(first - block, block - last), 0.0)
        felt = (gap < reach).astype(F32)
        rank = dot(jnp.broadcast_to(felt, (8, K)).astype(BF16), upper)[0:1]
        chosen = jnp.where(felt > 0.0, rank - 1.0, -1.0) == slots
        most = jnp.maximum(most, jnp.sum(felt).astype(I32))
        pick_ref[b] = ones_where(chosen)
        cols_ref[b, 0] = jnp.broadcast_to(column(chosen, block), (K, LB))
        cols_ref[b, 1] = jnp.broadcast_to(jnp.maximum(column(chosen, reach), 1.0), (K, LB))
        cols_ref[b, 2] = jnp.broadcast_to(column(chosen, damping), (K, LB))
    count_ref[0] = most
    distance = jnp.abs(blocks[1:2] - column(diagonal, blocks[0:1]))
    reach = column(diagonal, reaches[0:1])
    damping = column(diagonal, damp_ref[0:1, :])
    w_ref[...] = damping * jnp.maximum(0.0, 1.0 - distance / reach)


def places(sp, segment, place, damping, extent):
    return pl.pallas_call(
        places_kernel,
        grid_spec=pltpu.PrefetchScalarGridSpec(
            num_scalar_prefetch=1,
            grid=(1,),
            in_specs=[whole((B, K))] * 4,
            out_specs=[
                whole((B, K, K)),
                whole((B, 3, K, LB)),
                whole((K, K)),
                pl.BlockSpec(memory_space=pltpu.SMEM),
            ],
        ),
        out_shape=[
            jax.ShapeDtypeStruct((B, K, K), BF16),
            jax.ShapeDtypeStruct((B, 3, K, LB), F32),
            jax.ShapeDtypeStruct((K, K), F32),
            jax.ShapeDtypeStruct((1,), I32),
        ],
        compiler_params=pltpu.CompilerParams(vmem_limit_bytes=VMEM_LIMIT),
        cost_estimate=pl.CostEstimate(
            flops=1_000_000, bytes_accessed=2_000_000, transcendentals=0
        ),
        name="places",
    )(sp, segment, place, damping, extent)


def observe_stats(prior, values, variances):
    centre = jnp.sum(prior, axis=0, keepdims=True) / MEMBERS
    anomaly = prior - centre
    prior_var = jnp.sum(anomaly * anomaly, axis=0, keepdims=True) / (MEMBERS - 1) + 1e-06
    post_var = 1.0 / (1.0 / prior_var + 1.0 / variances)
    post_mean = post_var * (centre / prior_var + values / variances)
    shrink = jnp.sqrt(post_var / prior_var)
    increment = (post_mean - centre + (shrink - 1.0) * anomaly).astype(BF16)
    scaled = (anomaly * (1.0 / ((MEMBERS - 1) * prior_var))).astype(BF16)
    left = jnp.sum(scaled.astype(F32), axis=0, keepdims=True) * (-1.0 / EXTRA)
    return increment, jnp.concatenate([scaled, jnp.broadcast_to(left, (EXTRA, K)).astype(BF16)], 0)


def with_extra(x):
    return jnp.concatenate([x, x[:EXTRA]], 0)


def stats_kernel(mine_ref, other_ref, val_ref, var_ref, pick_ref, w_ref, cov_ref, chg_ref):
    def prior(b):
        at = slice(b * K, (b + 1) * K)
        return jnp.concatenate([mine_ref[:, at].astype(F32), other_ref[:, at].astype(F32)], 0)

    increment0, scaled0 = observe_stats(prior(0), val_ref[0:1, :], var_ref[0:1, :])
    before = prior(1)
    eye = ones_where(iota((K, K), 0) == iota((K, K), 1))
    cov = dot(dot_nt(eye, scaled0).astype(BF16), with_extra(before.astype(BF16)))
    gain = (w_ref[...] * cov).astype(BF16)
    after = (before + dot(increment0, gain)).astype(BF16).astype(F32)
    increment1, scaled1 = observe_stats(after, val_ref[1:2, :], var_ref[1:2, :])
    for b, (increment, scaled) in enumerate(((increment0, scaled0), (increment1, scaled1))):
        cov_ref[b] = dot_nt(pick_ref[b], scaled).astype(BF16)
        chg_ref[b] = dot_nt(increment, pick_ref[b]).astype(BF16)


def stats(mine, other, readings, spread, picks, w):
    return pl.pallas_call(
        stats_kernel,
        grid=(1,),
        in_specs=[
            whole((HALF, B * K)),
            whole((HALF, B * K)),
            whole((B, K)),
            whole((B, K)),
            whole((B, K, K)),
            whole((K, K)),
        ],
        out_specs=[whole((B, K, DEPTH)), whole((B, MEMBERS, K))],
        out_shape=[
            jax.ShapeDtypeStruct((B, K, DEPTH), BF16),
            jax.ShapeDtypeStruct((B, MEMBERS, K), BF16),
        ],
        compiler_params=pltpu.CompilerParams(vmem_limit_bytes=VMEM_LIMIT),
        name="stats",
    )(mine, other, readings, spread, picks, w)


def update_kernel(begin, sp_ref, count_ref, cov_ref, chg_ref, cols, mine_ref, other_ref, *rest):
    own_ref, away_ref = rest[-2:]
    step = pl.program_id(0) + begin
    first = sp_ref[1].astype(F32)

    def weights(b, kc):
        block = (first + (step * CHUNK_BLOCKS).astype(F32)) + iota((kc, LB), 1).astype(F32)
        distance = jnp.abs(block - cols[b, 0, :kc])
        return cols[b, 2, :kc] * jnp.maximum(0.0, 1.0 - distance / cols[b, 1, :kc])

    def advance(kc):
        w = [weights(b, kc) for b in range(B)]
        for group in range(CHUNK // (256 * GROUP)):
            pairs = range(group * GROUP, (group + 1) * GROUP)
            at = [slice(p * 256, (p + 1) * 256) for p in pairs]
            wide = [
                jnp.concatenate([mine_ref[:, a].astype(F32), other_ref[:, a].astype(F32)], 0)
                for a in at
            ]
            for b in range(B):
                cov = [dot(cov_ref[b, :kc], with_extra(x.astype(BF16))) for x in wide]
                gain = [
                    jnp.concatenate(
                        [
                            c[:, h * LB : (h + 1) * LB]
                            * jnp.broadcast_to(w[b][:, 2 * p + h : 2 * p + h + 1], (kc, LB))
                            for h in range(2)
                        ],
                        1,
                    ).astype(BF16)
                    for p, c in zip(pairs, cov)
                ]
                wide = [x + dot(chg_ref[b, :, :kc], g) for x, g in zip(wide, gain)]
                if b == 0:
                    wide = [x.astype(BF16).astype(F32) for x in wide]
            for a, x in zip(at, wide):
                own_ref[:, a] = x[:HALF].astype(BF16)
                away_ref[:, a] = x[HALF:].astype(BF16)

    n = count_ref[0]

    @pl.when(n <= 64)
    def _():
        advance(64)

    @pl.when((n > 64) & (n <= 128))
    def _():
        advance(128)

    @pl.when(n > 128)
    def _():
        advance(K)


def update(begin, steps, sp, count, cov, chg, cols, x, got, out):
    half = lambda i, s, c: (0, s[0] * STEPS + begin + i)
    in_specs = [
        whole((B, K, DEPTH)),
        whole((B, MEMBERS, K)),
        whole((B, 3, K, LB)),
        pl.BlockSpec((HALF, CHUNK), half),
        pl.BlockSpec((HALF, CHUNK), half),
    ]
    operands = [sp, count, cov, chg, cols, x, got]
    aliases = {}
    if out is not None:
        in_specs.append(pl.BlockSpec(memory_space=pl.ANY))
        operands.append(out)
        aliases = {len(operands) - 1: 0}
    return pl.pallas_call(
        lambda *refs: update_kernel(begin, *refs),
        grid_spec=pltpu.PrefetchScalarGridSpec(
            num_scalar_prefetch=2,
            grid=(steps,),
            in_specs=in_specs,
            out_specs=[
                pl.BlockSpec((HALF, CHUNK), half),
                pl.BlockSpec((HALF, CHUNK), lambda i, s, c: (0, i)),
            ],
        ),
        out_shape=[
            jax.ShapeDtypeStruct((HALF, CHIP), BF16),
            jax.ShapeDtypeStruct((HALF, steps * CHUNK), BF16),
        ],
        input_output_aliases=aliases,
        compiler_params=pltpu.CompilerParams(vmem_limit_bytes=VMEM_LIMIT),
        cost_estimate=pl.CostEstimate(
            flops=600_000_000 * steps,
            bytes_accessed=4 * MEMBERS * CHUNK * steps,
            transcendentals=0,
        ),
        name=f"update{begin}",
    )(*operands)


def fill_kernel(sp_ref, got_ref, out_hbm, out_ref):
    out_ref[...] = got_ref[...]


def fill(begin, steps, sp, got, out):
    return pl.pallas_call(
        fill_kernel,
        grid_spec=pltpu.PrefetchScalarGridSpec(
            num_scalar_prefetch=1,
            grid=(steps,),
            in_specs=[
                pl.BlockSpec((HALF, CHUNK), lambda i, s: (0, i)),
                pl.BlockSpec(memory_space=pl.ANY),
            ],
            out_specs=pl.BlockSpec(
                (HALF, CHUNK), lambda i, s: (0, (1 - s[0]) * STEPS + begin + i)
            ),
        ),
        out_shape=jax.ShapeDtypeStruct((HALF, CHIP), BF16),
        input_output_aliases={2: 0},
        compiler_params=pltpu.CompilerParams(vmem_limit_bytes=VMEM_LIMIT),
        name=f"fill{begin}",
    )(sp, got, out)


def shifted(array, by):
    pairs = [(i, (i + by) % CHIPS) for i in range(CHIPS)]
    return lax.ppermute(array, "state", pairs)


def swapped(array):
    return lax.ppermute(array, "mem", [(0, 1), (1, 0)])


def on_device(x, segment, place, readings, spread, damping, extent):
    core = lax.axis_index("mem")
    chip = lax.axis_index("state")
    sp = jnp.stack([core, (chip * 2 + core) * SEG_BLOCKS, chip]).astype(I32)

    picked = pick(sp, segment, place, x)
    x, picked = lax.optimization_barrier((x, picked))
    up, down = shifted(picked, 1), shifted(picked, -1)
    got = swapped(x)
    picks, cols, w, count = places(sp, segment, place, damping, extent)
    near = picked + up + down
    near, picks, cols, w, count = lax.optimization_barrier((near, picks, cols, w, count))
    far = near + shifted(near, 3) + shifted(near, -3)
    cov, chg = stats(far, swapped(far), readings, spread, picks, w)
    out = None
    away = []
    begin = 0
    for steps in PARTS:
        out, part = update(begin, steps, sp, count, cov, chg, cols, x, got, out)
        away.append((begin, steps, swapped(part)))
        begin += steps
    for begin, steps, part in away:
        out = fill(begin, steps, sp, part, out)
    return out


def solution(mesh):
    in_specs = (P("mem", "state"), P(), P(), P(), P(), P(), P())
    return jax.shard_map(
        on_device, mesh=mesh, in_specs=in_specs, out_specs=P("mem", "state"), check_vma=False
    )
```

```python
import jax
import jax.numpy as jnp
from jax import lax
from jax.experimental import pallas as pl
from jax.experimental.pallas import tpu as pltpu
from jax.sharding import PartitionSpec as P

MEMBERS = 80
HALF = 40
SD = 32768
K = 256
B = 2
LB = 128
CHIP = 2 * SD
CHIPS = 64
SEG_BLOCKS = SD // LB
CHUNK = 2048
STEPS = SD // CHUNK
CHUNK_BLOCKS = CHUNK // LB
PARTS = (7, 6, 3)
GROUP = 4
EXTRA = 16
DEPTH = MEMBERS + EXTRA
F32 = jnp.float32
BF16 = jnp.bfloat16
I32 = jnp.int32
NT = (((1,), (1,)), ((), ()))
VMEM_LIMIT = 40 * 1024 * 1024
PICK_LIMIT = 40 * 1024 * 1024


def dot(a, b):
    return jnp.dot(a, b, preferred_element_type=F32)


def dot_nt(a, b):
    return lax.dot_general(a, b, NT, preferred_element_type=F32)


def iota(shape, dim):
    return lax.broadcasted_iota(I32, shape, dim)


def ones_where(mask):
    return mask.astype(F32).astype(BF16)


def whole(shape):
    return pl.BlockSpec(shape, lambda i, *s: (0,) * len(shape))


def pick_kernel(sp_ref, index_ref, x_ref, o_ref, xv, acc, owned, sems):
    parts = 4
    width = CHIP // parts
    copies = [
        pltpu.make_async_copy(
            x_ref.at[:, pl.ds(p * width, width)], xv.at[:, pl.ds(p * width, width)], sems.at[p]
        )
        for p in range(parts)
    ]
    for copy in copies:
        copy.start()
    acc[...] = jnp.zeros_like(acc)
    chip = sp_ref[2]
    n = I32(0)
    for b in range(B):

        def scan(k, n, b=b):
            owned[n] = b * K + k
            return n + ((index_ref[b, k] >> 16) == chip).astype(I32)

        n = lax.fori_loop(0, K, scan, n, unroll=16)
    for j in range(4):
        owned[n + j] = B * K
    for copy in copies:
        copy.wait()
    lane = iota((HALF, LB), 1)

    def extract(i, _):
        for j in range(4):
            k = owned[4 * i + j]
            b = jnp.minimum(k >> 8, B - 1)
            within = k & (K - 1)
            at = index_ref[b, within] & (CHIP - 1)
            start = pl.multiple_of((at >> 7) * LB, LB)
            tile = xv[:, pl.ds(start, LB)].astype(F32)
            turned = pltpu.roll(tile, (k - at) & (LB - 1), 1)
            pltpu.store(acc.at[k >> 7], turned, mask=lane == (k & (LB - 1)))
        return 0

    lax.fori_loop(0, (n + 3) >> 2, extract, 0)
    for g in range(B * K // LB):
        o_ref[:, g * LB : (g + 1) * LB] = acc[g].astype(BF16)


def pick(sp, index, x):
    return pl.pallas_call(
        pick_kernel,
        grid_spec=pltpu.PrefetchScalarGridSpec(
            num_scalar_prefetch=2,
            grid=(1,),
            in_specs=[pl.BlockSpec(memory_space=pl.ANY)],
            out_specs=whole((HALF, B * K)),
            scratch_shapes=[
                pltpu.VMEM((HALF, CHIP), BF16),
                pltpu.VMEM((B * K // LB + 1, HALF, LB), F32),
                pltpu.SMEM((B * K + 8,), I32),
                pltpu.SemaphoreType.DMA((4,)),
            ],
        ),
        out_shape=jax.ShapeDtypeStruct((HALF, B * K), BF16),
        compiler_params=pltpu.CompilerParams(vmem_limit_bytes=PICK_LIMIT),
        cost_estimate=pl.CostEstimate(flops=0, bytes_accessed=2 * HALF * CHIP, transcendentals=0),
        name="pick",
    )(sp, index, x)


def places_kernel(
    sp_ref, seg_ref, place_ref, damp_ref, ext_ref, pick_ref, cols_ref, w_ref, count_ref
):
    first = sp_ref[1].astype(F32)
    last = first + (SEG_BLOCKS - 1)
    blocks = (seg_ref[...] * SEG_BLOCKS + (place_ref[...] >> 7)).astype(F32)
    reaches = ext_ref[...].astype(F32) + 1.0
    diagonal = iota((K, K), 0) == iota((K, K), 1)
    upper = ones_where(iota((K, K), 0) <= iota((K, K), 1))
    slots = iota((K, K), 0).astype(F32)
    most = I32(0)

    def column(mask, row):
        return jnp.sum(jnp.where(mask, row, 0.0), axis=1, keepdims=True)

    for b in range(B):
        block, reach, damping = blocks[b : b + 1], reaches[b : b + 1], damp_ref[b : b + 1, :]
        gap = jnp.maximum(jnp.maximum(first - block, block - last), 0.0)
        felt = (gap < reach).astype(F32)
        rank = dot(jnp.broadcast_to(felt, (8, K)).astype(BF16), upper)[0:1]
        chosen = jnp.where(felt > 0.0, rank - 1.0, -1.0) == slots
        most = jnp.maximum(most, jnp.sum(felt).astype(I32))
        pick_ref[b] = ones_where(chosen)
        cols_ref[b, 0] = jnp.broadcast_to(column(chosen, block), (K, LB))
        cols_ref[b, 1] = jnp.broadcast_to(jnp.maximum(column(chosen, reach), 1.0), (K, LB))
        cols_ref[b, 2] = jnp.broadcast_to(column(chosen, damping), (K, LB))
    count_ref[0] = most
    distance = jnp.abs(blocks[1:2] - column(diagonal, blocks[0:1]))
    reach = column(diagonal, reaches[0:1])
    damping = column(diagonal, damp_ref[0:1, :])
    w_ref[...] = damping * jnp.maximum(0.0, 1.0 - distance / reach)


def places(sp, segment, place, damping, extent):
    return pl.pallas_call(
        places_kernel,
        grid_spec=pltpu.PrefetchScalarGridSpec(
            num_scalar_prefetch=1,
            grid=(1,),
            in_specs=[whole((B, K))] * 4,
            out_specs=[
                whole((B, K, K)),
                whole((B, 3, K, LB)),
                whole((K, K)),
                pl.BlockSpec(memory_space=pltpu.SMEM),
            ],
        ),
        out_shape=[
            jax.ShapeDtypeStruct((B, K, K), BF16),
            jax.ShapeDtypeStruct((B, 3, K, LB), F32),
            jax.ShapeDtypeStruct((K, K), F32),
            jax.ShapeDtypeStruct((1,), I32),
        ],
        compiler_params=pltpu.CompilerParams(vmem_limit_bytes=VMEM_LIMIT),
        cost_estimate=pl.CostEstimate(
            flops=1_000_000, bytes_accessed=2_000_000, transcendentals=0
        ),
        name="places",
    )(sp, segment, place, damping, extent)


def observe_stats(prior, values, variances):
    centre = jnp.sum(prior, axis=0, keepdims=True) / MEMBERS
    anomaly = prior - centre
    prior_var = jnp.sum(anomaly * anomaly, axis=0, keepdims=True) / (MEMBERS - 1) + 1e-06
    post_var = 1.0 / (1.0 / prior_var + 1.0 / variances)
    post_mean = post_var * (centre / prior_var + values / variances)
    shrink = jnp.sqrt(post_var / prior_var)
    increment = (post_mean - centre + (shrink - 1.0) * anomaly).astype(BF16)
    scaled = (anomaly * (1.0 / ((MEMBERS - 1) * prior_var))).astype(BF16)
    left = jnp.sum(scaled.astype(F32), axis=0, keepdims=True) * (-1.0 / EXTRA)
    return increment, jnp.concatenate([scaled, jnp.broadcast_to(left, (EXTRA, K)).astype(BF16)], 0)


def with_extra(x):
    return jnp.concatenate([x, x[:EXTRA]], 0)


def stats_kernel(mine_ref, other_ref, val_ref, var_ref, pick_ref, w_ref, cov_ref, chg_ref):
    def prior(b):
        at = slice(b * K, (b + 1) * K)
        return jnp.concatenate([mine_ref[:, at].astype(F32), other_ref[:, at].astype(F32)], 0)

    increment0, scaled0 = observe_stats(prior(0), val_ref[0:1, :], var_ref[0:1, :])
    before = prior(1)
    eye = ones_where(iota((K, K), 0) == iota((K, K), 1))
    cov = dot(dot_nt(eye, scaled0).astype(BF16), with_extra(before.astype(BF16)))
    gain = (w_ref[...] * cov).astype(BF16)
    after = (before + dot(increment0, gain)).astype(BF16).astype(F32)
    increment1, scaled1 = observe_stats(after, val_ref[1:2, :], var_ref[1:2, :])
    for b, (increment, scaled) in enumerate(((increment0, scaled0), (increment1, scaled1))):
        cov_ref[b] = dot_nt(pick_ref[b], scaled).astype(BF16)
        chg_ref[b] = dot_nt(increment, pick_ref[b]).astype(BF16)


def stats(mine, other, readings, spread, picks, w):
    return pl.pallas_call(
        stats_kernel,
        grid=(1,),
        in_specs=[
            whole((HALF, B * K)),
            whole((HALF, B * K)),
            whole((B, K)),
            whole((B, K)),
            whole((B, K, K)),
            whole((K, K)),
        ],
        out_specs=[whole((B, K, DEPTH)), whole((B, MEMBERS, K))],
        out_shape=[
            jax.ShapeDtypeStruct((B, K, DEPTH), BF16),
            jax.ShapeDtypeStruct((B, MEMBERS, K), BF16),
        ],
        compiler_params=pltpu.CompilerParams(vmem_limit_bytes=VMEM_LIMIT),
        name="stats",
    )(mine, other, readings, spread, picks, w)


def update_kernel(begin, sp_ref, count_ref, cov_ref, chg_ref, cols, mine_ref, other_ref, *rest):
    own_ref, away_ref = rest[-2:]
    step = pl.program_id(0) + begin
    first = sp_ref[1].astype(F32)

    def weights(b, kc):
        block = (first + (step * CHUNK_BLOCKS).astype(F32)) + iota((kc, LB), 1).astype(F32)
        distance = jnp.abs(block - cols[b, 0, :kc])
        return cols[b, 2, :kc] * jnp.maximum(0.0, 1.0 - distance / cols[b, 1, :kc])

    def advance(kc):
        w = [weights(b, kc) for b in range(B)]
        for group in range(CHUNK // (256 * GROUP)):
            pairs = range(group * GROUP, (group + 1) * GROUP)
            at = [slice(p * 256, (p + 1) * 256) for p in pairs]
            wide = [
                jnp.concatenate([mine_ref[:, a].astype(F32), other_ref[:, a].astype(F32)], 0)
                for a in at
            ]
            for b in range(B):
                cov = [dot(cov_ref[b, :kc], with_extra(x.astype(BF16))) for x in wide]
                gain = [
                    jnp.concatenate(
                        [
                            c[:, h * LB : (h + 1) * LB]
                            * jnp.broadcast_to(w[b][:, 2 * p + h : 2 * p + h + 1], (kc, LB))
                            for h in range(2)
                        ],
                        1,
                    ).astype(BF16)
                    for p, c in zip(pairs, cov)
                ]
                wide = [x + dot(chg_ref[b, :, :kc], g) for x, g in zip(wide, gain)]
                if b == 0:
                    wide = [x.astype(BF16).astype(F32) for x in wide]
            for a, x in zip(at, wide):
                own_ref[:, a] = x[:HALF].astype(BF16)
                away_ref[:, a] = x[HALF:].astype(BF16)

    n = count_ref[0]

    @pl.when(n <= 32)
    def _():
        advance(32)

    @pl.when((n > 32) & (n <= 64))
    def _():
        advance(64)

    @pl.when((n > 64) & (n <= 128))
    def _():
        advance(128)

    @pl.when(n > 128)
    def _():
        advance(K)


def update(begin, steps, sp, count, cov, chg, cols, x, got, out):
    half = lambda i, s, c: (0, s[0] * STEPS + begin + i)
    in_specs = [pl.BlockSpec(memory_space=pltpu.VMEM)] * 3 + [
        pl.BlockSpec((HALF, CHUNK), half),
        pl.BlockSpec((HALF, CHUNK), half),
    ]
    operands = [sp, count, cov, chg, cols, x, got]
    aliases = {}
    if out is not None:
        in_specs.append(pl.BlockSpec(memory_space=pl.ANY))
        operands.append(out)
        aliases = {len(operands) - 1: 0}
    return pl.pallas_call(
        lambda *refs: update_kernel(begin, *refs),
        grid_spec=pltpu.PrefetchScalarGridSpec(
            num_scalar_prefetch=2,
            grid=(steps,),
            in_specs=in_specs,
            out_specs=[
                pl.BlockSpec((HALF, CHUNK), half),
                pl.BlockSpec((HALF, CHUNK), lambda i, s, c: (0, i)),
            ],
        ),
        out_shape=[
            jax.ShapeDtypeStruct((HALF, CHIP), BF16),
            jax.ShapeDtypeStruct((HALF, steps * CHUNK), BF16),
        ],
        input_output_aliases=aliases,
        compiler_params=pltpu.CompilerParams(vmem_limit_bytes=VMEM_LIMIT),
        cost_estimate=pl.CostEstimate(
            flops=600_000_000 * steps,
            bytes_accessed=4 * MEMBERS * CHUNK * steps,
            transcendentals=0,
        ),
        name=f"update{begin}",
    )(*operands)


def fill(begins, sp, parts, out):
    def kernel(sp_ref, *refs):
        out_ref, sems = refs[-2:]
        base = (1 - sp_ref[0]) * SD
        copies = []
        for j, (begin, part) in enumerate(zip(begins, refs[: len(parts)])):
            start = pl.multiple_of(base + begin * CHUNK, CHUNK)
            to = out_ref.at[:, pl.ds(start, part.shape[1])]
            copies.append(pltpu.make_async_copy(part, to, sems.at[j]))
        for copy in copies:
            copy.start()
        for copy in copies:
            copy.wait()

    return pl.pallas_call(
        kernel,
        grid_spec=pltpu.PrefetchScalarGridSpec(
            num_scalar_prefetch=1,
            grid=(1,),
            in_specs=[pl.BlockSpec(memory_space=pltpu.VMEM)] * len(parts)
            + [pl.BlockSpec(memory_space=pl.ANY)],
            out_specs=pl.BlockSpec(memory_space=pl.ANY),
            scratch_shapes=[pltpu.SemaphoreType.DMA((len(parts),))],
        ),
        out_shape=jax.ShapeDtypeStruct((HALF, CHIP), BF16),
        input_output_aliases={1 + len(parts): 0},
        compiler_params=pltpu.CompilerParams(vmem_limit_bytes=VMEM_LIMIT),
        name=f"fill{begins[0]}",
    )(sp, *parts, out)


def sent(array, target):
    return lax.ppermute(array, "state", [(i, target(i)) for i in range(CHIPS)])


def along_row(array, by):
    return sent(array, lambda i: i // 4 * 4 + (i + by) % 4)


def across_rows(array, by):
    return sent(array, lambda i: (i + 4 * by) % CHIPS)


def swapped(array):
    return lax.ppermute(array, "mem", [(0, 1), (1, 0)])


def on_device(x, segment, place, readings, spread, damping, extent):
    core = lax.axis_index("mem")
    chip = lax.axis_index("state")
    sp = jnp.stack([core, (chip * 2 + core) * SEG_BLOCKS, chip]).astype(I32)

    picked = pick(sp, segment * SD + place, x)
    x, picked = lax.optimization_barrier((x, picked))
    two, one, three = (along_row(picked, by) for by in (2, 1, 3))
    got = swapped(x)
    picks, cols, w, count = places(sp, segment, place, damping, extent)
    near = picked + one + two + three
    near, picks, cols, w, count = lax.optimization_barrier((near, picks, cols, w, count))
    far = near + across_rows(near, 1) + across_rows(near, -1)
    cov, chg = stats(far, swapped(far), readings, spread, picks, w)
    out = None
    away = []
    begin = 0
    for steps in PARTS:
        out, part = update(begin, steps, sp, count, cov, chg, cols, x, got, out)
        away.append((begin, swapped(part)))
        begin += steps
    for some in (away[:-1], away[-1:]):
        out = fill([begin for begin, _ in some], sp, [part for _, part in some], out)
    return out


def solution(mesh):
    in_specs = (P("mem", "state"), P(), P(), P(), P(), P(), P())
    return jax.shard_map(
        on_device, mesh=mesh, in_specs=in_specs, out_specs=P("mem", "state"), check_vma=False
    )
```

```python
import jax
import jax.numpy as jnp
from jax import lax
from jax.experimental import pallas as pl
from jax.experimental.pallas import tpu as pltpu
from jax.sharding import PartitionSpec as P

MEMBERS = 80
HALF = 40
SD = 32768
K = 256
B = 2
LB = 128
CHIP = 2 * SD
CHIPS = 64
SEG_BLOCKS = SD // LB
CHUNK = 2048
STEPS = SD // CHUNK
CHUNK_BLOCKS = CHUNK // LB
PARTS = (11, 5)
GROUP = 4
FLIGHT = 16
EXTRA = 16
DEPTH = MEMBERS + EXTRA
F32 = jnp.float32
BF16 = jnp.bfloat16
I32 = jnp.int32
NT = (((1,), (1,)), ((), ()))
VMEM_LIMIT = 40 * 1024 * 1024
PICK_LIMIT = 40 * 1024 * 1024


def dot(a, b):
    return jnp.dot(a, b, preferred_element_type=F32)


def dot_nt(a, b):
    return lax.dot_general(a, b, NT, preferred_element_type=F32)


def iota(shape, dim):
    return lax.broadcasted_iota(I32, shape, dim)


def ones_where(mask):
    return mask.astype(F32).astype(BF16)


def whole(shape):
    return pl.BlockSpec(shape, lambda i, *s: (0,) * len(shape))


def pick_kernel(sp_ref, index_ref, x_ref, o_ref, xv, acc, owned, sems):
    parts = 4
    width = CHIP // parts
    copies = [
        pltpu.make_async_copy(
            x_ref.at[:, pl.ds(p * width, width)], xv.at[:, pl.ds(p * width, width)], sems.at[p]
        )
        for p in range(parts)
    ]
    for copy in copies:
        copy.start()
    acc[...] = jnp.zeros_like(acc)
    chip = sp_ref[2]
    n = I32(0)
    for b in range(B):

        def scan(k, n, b=b):
            owned[n] = b * K + k
            return n + ((index_ref[b, k] >> 16) == chip).astype(I32)

        n = lax.fori_loop(0, K, scan, n, unroll=16)
    for j in range(FLIGHT):
        owned[n + j] = B * K
    for copy in copies:
        copy.wait()
    lane = iota((HALF, LB), 1)

    def extract(i, _):
        for j in range(FLIGHT):
            k = owned[FLIGHT * i + j]
            b = jnp.minimum(k >> 8, B - 1)
            within = k & (K - 1)
            at = index_ref[b, within] & (CHIP - 1)
            start = pl.multiple_of((at >> 7) * LB, LB)
            tile = xv[:, pl.ds(start, LB)].astype(F32)
            turned = pltpu.roll(tile, (k - at) & (LB - 1), 1)
            pltpu.store(acc.at[k >> 7], turned, mask=lane == (k & (LB - 1)))
        return 0

    lax.fori_loop(0, (n + FLIGHT - 1) // FLIGHT, extract, 0)
    for g in range(B * K // LB):
        o_ref[:, g * LB : (g + 1) * LB] = acc[g].astype(BF16)


def pick(sp, index, x):
    return pl.pallas_call(
        pick_kernel,
        grid_spec=pltpu.PrefetchScalarGridSpec(
            num_scalar_prefetch=2,
            grid=(1,),
            in_specs=[pl.BlockSpec(memory_space=pl.ANY)],
            out_specs=whole((HALF, B * K)),
            scratch_shapes=[
                pltpu.VMEM((HALF, CHIP), BF16),
                pltpu.VMEM((B * K // LB + 1, HALF, LB), F32),
                pltpu.SMEM((B * K + FLIGHT,), I32),
                pltpu.SemaphoreType.DMA((4,)),
            ],
        ),
        out_shape=jax.ShapeDtypeStruct((HALF, B * K), BF16),
        compiler_params=pltpu.CompilerParams(vmem_limit_bytes=PICK_LIMIT),
        cost_estimate=pl.CostEstimate(flops=0, bytes_accessed=2 * HALF * CHIP, transcendentals=0),
        name="pick",
    )(sp, index, x)


def places_kernel(
    sp_ref, seg_ref, place_ref, damp_ref, ext_ref, pick_ref, cols_ref, w_ref, count_ref
):
    first = sp_ref[1].astype(F32)
    last = first + (SEG_BLOCKS - 1)
    blocks = (seg_ref[...] * SEG_BLOCKS + (place_ref[...] >> 7)).astype(F32)
    reaches = ext_ref[...].astype(F32) + 1.0
    diagonal = iota((K, K), 0) == iota((K, K), 1)
    upper = ones_where(iota((K, K), 0) <= iota((K, K), 1))
    slots = iota((K, K), 0).astype(F32)
    most = I32(0)

    def column(mask, row):
        return jnp.sum(jnp.where(mask, row, 0.0), axis=1, keepdims=True)

    for b in range(B):
        block, reach, damping = blocks[b : b + 1], reaches[b : b + 1], damp_ref[b : b + 1, :]
        gap = jnp.maximum(jnp.maximum(first - block, block - last), 0.0)
        felt = (gap < reach).astype(F32)
        rank = dot(jnp.broadcast_to(felt, (8, K)).astype(BF16), upper)[0:1]
        chosen = jnp.where(felt > 0.0, rank - 1.0, -1.0) == slots
        most = jnp.maximum(most, jnp.sum(felt).astype(I32))
        pick_ref[b] = ones_where(chosen)
        cols_ref[b, 0] = jnp.broadcast_to(column(chosen, block), (K, LB))
        cols_ref[b, 1] = jnp.broadcast_to(jnp.maximum(column(chosen, reach), 1.0), (K, LB))
        cols_ref[b, 2] = jnp.broadcast_to(column(chosen, damping), (K, LB))
    count_ref[0] = most
    distance = jnp.abs(blocks[1:2] - column(diagonal, blocks[0:1]))
    reach = column(diagonal, reaches[0:1])
    damping = column(diagonal, damp_ref[0:1, :])
    w_ref[...] = damping * jnp.maximum(0.0, 1.0 - distance / reach)


def places(sp, segment, place, damping, extent):
    return pl.pallas_call(
        places_kernel,
        grid_spec=pltpu.PrefetchScalarGridSpec(
            num_scalar_prefetch=1,
            grid=(1,),
            in_specs=[whole((B, K))] * 4,
            out_specs=[
                whole((B, K, K)),
                whole((B, 3, K, LB)),
                whole((K, K)),
                pl.BlockSpec(memory_space=pltpu.SMEM),
            ],
        ),
        out_shape=[
            jax.ShapeDtypeStruct((B, K, K), BF16),
            jax.ShapeDtypeStruct((B, 3, K, LB), F32),
            jax.ShapeDtypeStruct((K, K), F32),
            jax.ShapeDtypeStruct((1,), I32),
        ],
        compiler_params=pltpu.CompilerParams(vmem_limit_bytes=VMEM_LIMIT),
        cost_estimate=pl.CostEstimate(
            flops=1_000_000, bytes_accessed=2_000_000, transcendentals=0
        ),
        name="places",
    )(sp, segment, place, damping, extent)


def observe_stats(prior, values, variances):
    centre = jnp.sum(prior, axis=0, keepdims=True) / MEMBERS
    anomaly = prior - centre
    prior_var = jnp.sum(anomaly * anomaly, axis=0, keepdims=True) / (MEMBERS - 1) + 1e-06
    post_var = 1.0 / (1.0 / prior_var + 1.0 / variances)
    post_mean = post_var * (centre / prior_var + values / variances)
    shrink = jnp.sqrt(post_var / prior_var)
    increment = (post_mean - centre + (shrink - 1.0) * anomaly).astype(BF16)
    scaled = (anomaly * (1.0 / ((MEMBERS - 1) * prior_var))).astype(BF16)
    left = jnp.sum(scaled.astype(F32), axis=0, keepdims=True) * (-1.0 / EXTRA)
    return increment, jnp.concatenate([scaled, jnp.broadcast_to(left, (EXTRA, K)).astype(BF16)], 0)


def with_extra(x):
    return jnp.concatenate([x, x[:EXTRA]], 0)


def stats_kernel(mine_ref, other_ref, val_ref, var_ref, pick_ref, w_ref, cov_ref, chg_ref):
    def prior(b):
        at = slice(b * K, (b + 1) * K)
        return jnp.concatenate([mine_ref[:, at].astype(F32), other_ref[:, at].astype(F32)], 0)

    increment0, scaled0 = observe_stats(prior(0), val_ref[0:1, :], var_ref[0:1, :])
    before = prior(1)
    eye = ones_where(iota((K, K), 0) == iota((K, K), 1))
    cov = dot(dot_nt(eye, scaled0).astype(BF16), with_extra(before.astype(BF16)))
    gain = (w_ref[...] * cov).astype(BF16)
    after = (before + dot(increment0, gain)).astype(BF16).astype(F32)
    increment1, scaled1 = observe_stats(after, val_ref[1:2, :], var_ref[1:2, :])
    for b, (increment, scaled) in enumerate(((increment0, scaled0), (increment1, scaled1))):
        cov_ref[b] = dot_nt(pick_ref[b], scaled).astype(BF16)
        chg_ref[b] = dot_nt(increment, pick_ref[b]).astype(BF16)


def stats(mine, other, readings, spread, picks, w):
    return pl.pallas_call(
        stats_kernel,
        grid=(1,),
        in_specs=[
            whole((HALF, B * K)),
            whole((HALF, B * K)),
            whole((B, K)),
            whole((B, K)),
            whole((B, K, K)),
            whole((K, K)),
        ],
        out_specs=[whole((B, K, DEPTH)), whole((B, MEMBERS, K))],
        out_shape=[
            jax.ShapeDtypeStruct((B, K, DEPTH), BF16),
            jax.ShapeDtypeStruct((B, MEMBERS, K), BF16),
        ],
        compiler_params=pltpu.CompilerParams(vmem_limit_bytes=VMEM_LIMIT),
        name="stats",
    )(mine, other, readings, spread, picks, w)


def moved(base, a):
    return pl.ds(pl.multiple_of(base + a.start, 256), 256)


def update_kernel(begin, sp_ref, count_ref, cov_ref, chg_ref, cols, mine_ref, other_ref, *rest):
    own_ref, away_ref = rest[-2:]
    step = pl.program_id(0) + begin
    there = sp_ref[0] * SD + step * CHUNK
    back = pl.program_id(0) * CHUNK
    first = sp_ref[1].astype(F32)

    def weights(b, kc):
        block = (first + (step * CHUNK_BLOCKS).astype(F32)) + iota((kc, LB), 1).astype(F32)
        distance = jnp.abs(block - cols[b, 0, :kc])
        return cols[b, 2, :kc] * jnp.maximum(0.0, 1.0 - distance / cols[b, 1, :kc])

    def advance(kc):
        w = [weights(b, kc) for b in range(B)]
        for group in range(CHUNK // (256 * GROUP)):
            pairs = range(group * GROUP, (group + 1) * GROUP)
            at = [slice(p * 256, (p + 1) * 256) for p in pairs]
            wide = [
                jnp.concatenate(
                    [mine_ref[:, a].astype(F32), other_ref[:, moved(there, a)].astype(F32)], 0
                )
                for a in at
            ]
            for b in range(B):
                cov = [dot(cov_ref[b, :kc], with_extra(x.astype(BF16))) for x in wide]
                gain = [
                    jnp.concatenate(
                        [
                            c[:, h * LB : (h + 1) * LB]
                            * jnp.broadcast_to(w[b][:, 2 * p + h : 2 * p + h + 1], (kc, LB))
                            for h in range(2)
                        ],
                        1,
                    ).astype(BF16)
                    for p, c in zip(pairs, cov)
                ]
                wide = [x + dot(chg_ref[b, :, :kc], g) for x, g in zip(wide, gain)]
                if b == 0:
                    wide = [x.astype(BF16).astype(F32) for x in wide]
            for a, x in zip(at, wide):
                own_ref[:, a] = x[:HALF].astype(BF16)
                away_ref[:, moved(back, a)] = x[HALF:].astype(BF16)

    n = count_ref[0]

    @pl.when(n <= 32)
    def _():
        advance(32)

    @pl.when((n > 32) & (n <= 64))
    def _():
        advance(64)

    @pl.when((n > 64) & (n <= 128))
    def _():
        advance(128)

    @pl.when(n > 128)
    def _():
        advance(K)


def update(begin, steps, sp, count, cov, chg, cols, x, got, out):
    half = lambda i, s, c: (0, s[0] * STEPS + begin + i)
    in_specs = [pl.BlockSpec(memory_space=pltpu.VMEM)] * 3 + [
        pl.BlockSpec((HALF, CHUNK), half),
        pl.BlockSpec(memory_space=pltpu.VMEM),
    ]
    operands = [sp, count, cov, chg, cols, x, got]
    aliases = {}
    if out is not None:
        in_specs.append(pl.BlockSpec(memory_space=pl.ANY))
        operands.append(out)
        aliases = {len(operands) - 1: 0}
    return pl.pallas_call(
        lambda *refs: update_kernel(begin, *refs),
        grid_spec=pltpu.PrefetchScalarGridSpec(
            num_scalar_prefetch=2,
            grid=(steps,),
            in_specs=in_specs,
            out_specs=[
                pl.BlockSpec((HALF, CHUNK), half),
                pl.BlockSpec(memory_space=pltpu.VMEM),
            ],
        ),
        out_shape=[
            jax.ShapeDtypeStruct((HALF, CHIP), BF16),
            jax.ShapeDtypeStruct((HALF, steps * CHUNK), BF16),
        ],
        input_output_aliases=aliases,
        compiler_params=pltpu.CompilerParams(vmem_limit_bytes=VMEM_LIMIT),
        cost_estimate=pl.CostEstimate(
            flops=600_000_000 * steps,
            bytes_accessed=4 * MEMBERS * CHUNK * steps,
            transcendentals=0,
        ),
        name=f"update{begin}",
    )(*operands)


def fill(begins, sp, parts, out):
    def kernel(sp_ref, *refs):
        out_ref, sems = refs[-2:]
        base = (1 - sp_ref[0]) * SD
        copies = []
        for j, (begin, part) in enumerate(zip(begins, refs[: len(parts)])):
            start = pl.multiple_of(base + begin * CHUNK, CHUNK)
            to = out_ref.at[:, pl.ds(start, part.shape[1])]
            copies.append(pltpu.make_async_copy(part, to, sems.at[j]))
        for copy in copies:
            copy.start()
        for copy in copies:
            copy.wait()

    return pl.pallas_call(
        kernel,
        grid_spec=pltpu.PrefetchScalarGridSpec(
            num_scalar_prefetch=1,
            grid=(1,),
            in_specs=[pl.BlockSpec(memory_space=pltpu.VMEM)] * len(parts)
            + [pl.BlockSpec(memory_space=pl.ANY)],
            out_specs=pl.BlockSpec(memory_space=pl.ANY),
            scratch_shapes=[pltpu.SemaphoreType.DMA((len(parts),))],
        ),
        out_shape=jax.ShapeDtypeStruct((HALF, CHIP), BF16),
        input_output_aliases={1 + len(parts): 0},
        compiler_params=pltpu.CompilerParams(vmem_limit_bytes=VMEM_LIMIT),
        name=f"fill{begins[0]}",
    )(sp, *parts, out)


def sent(array, target):
    pairs = [(i, target(i)) for i in range(CHIPS)]
    return lax.ppermute(array, "state", [(i, j) for i, j in pairs if 0 <= j < CHIPS])


def along_row(array, by):
    return sent(array, lambda i: i // 4 * 4 + (i + by) % 4)


def across_rows(array, by):
    return sent(array, lambda i: i + 4 * by)


def swapped(array):
    return lax.ppermute(array, "mem", [(0, 1), (1, 0)])


def on_device(x, segment, place, readings, spread, damping, extent):
    core = lax.axis_index("mem")
    chip = lax.axis_index("state")
    sp = jnp.stack([core, (chip * 2 + core) * SEG_BLOCKS, chip]).astype(I32)

    picked = pick(sp, segment * SD + place, x)
    x, picked = lax.optimization_barrier((x, picked))
    two, one, three = (along_row(picked, by) for by in (2, 1, 3))
    got = swapped(x)
    picks, cols, w, count = places(sp, segment, place, damping, extent)
    near = picked + one + two + three
    near, picks, cols, w, count = lax.optimization_barrier((near, picks, cols, w, count))
    far = near + across_rows(near, 1) + across_rows(near, -1)
    cov, chg = stats(far, swapped(far), readings, spread, picks, w)
    out = None
    away = []
    begin = 0
    for steps in PARTS:
        out, part = update(begin, steps, sp, count, cov, chg, cols, x, got, out)
        away.append((begin, swapped(part)))
        begin += steps
    for some in (away[:-1], away[-1:]):
        out = fill([begin for begin, _ in some], sp, [part for _, part in some], out)
    return out


def solution(mesh):
    in_specs = (P("mem", "state"), P(), P(), P(), P(), P(), P())
    return jax.shard_map(
        on_device, mesh=mesh, in_specs=in_specs, out_specs=P("mem", "state"), check_vma=False
    )
```

```python
import jax
import jax.numpy as jnp
from jax import lax
from jax.experimental import pallas as pl
from jax.experimental.pallas import tpu as pltpu
from jax.sharding import PartitionSpec as P

MEMBERS = 80
HALF = 40
SD = 32768
K = 256
B = 2
LB = 128
CHIP = 2 * SD
CHIPS = 64
SEG_BLOCKS = SD // LB
CHUNK = 4096
STEPS = SD // CHUNK
CHUNK_BLOCKS = CHUNK // LB
PARTS = (6, 2)
IN_FLIGHT = {32: 16, 64: 16, 128: 8, K: 4}
PIECES = 4
FLIGHT = 16
EXTRA = 16
DEPTH = MEMBERS + EXTRA
F32 = jnp.float32
BF16 = jnp.bfloat16
I32 = jnp.int32
NT = (((1,), (1,)), ((), ()))
VMEM_LIMIT = 40 * 1024 * 1024
PICK_LIMIT = 40 * 1024 * 1024


def dot(a, b):
    return jnp.dot(a, b, preferred_element_type=F32)


def dot_nt(a, b):
    return lax.dot_general(a, b, NT, preferred_element_type=F32)


def iota(shape, dim):
    return lax.broadcasted_iota(I32, shape, dim)


def ones_where(mask):
    return mask.astype(F32).astype(BF16)


def whole(shape):
    return pl.BlockSpec(shape, lambda i, *s: (0,) * len(shape))


def pick_kernel(sp_ref, index_ref, x_ref, o_ref, xv, acc, owned, sems):
    parts = 4
    width = CHIP // parts
    copies = [
        pltpu.make_async_copy(
            x_ref.at[:, pl.ds(p * width, width)], xv.at[:, pl.ds(p * width, width)], sems.at[p]
        )
        for p in range(parts)
    ]
    for copy in copies:
        copy.start()
    acc[...] = jnp.zeros_like(acc)
    chip = sp_ref[2]
    n = I32(0)
    for b in range(B):

        def scan(k, n, b=b):
            owned[n] = b * K + k
            return n + ((index_ref[b, k] >> 16) == chip).astype(I32)

        n = lax.fori_loop(0, K, scan, n, unroll=16)
    for j in range(FLIGHT):
        owned[n + j] = B * K
    for copy in copies:
        copy.wait()
    lane = iota((HALF, LB), 1)

    def extract(i, _):
        for j in range(FLIGHT):
            k = owned[FLIGHT * i + j]
            b = jnp.minimum(k >> 8, B - 1)
            within = k & (K - 1)
            at = index_ref[b, within] & (CHIP - 1)
            start = pl.multiple_of((at >> 7) * LB, LB)
            tile = xv[:, pl.ds(start, LB)].astype(F32)
            turned = pltpu.roll(tile, (k - at) & (LB - 1), 1)
            pltpu.store(acc.at[k >> 7], turned, mask=lane == (k & (LB - 1)))
        return 0

    lax.fori_loop(0, (n + FLIGHT - 1) // FLIGHT, extract, 0)
    for g in range(B * K // LB):
        o_ref[:, g * LB : (g + 1) * LB] = acc[g].astype(BF16)


def pick(sp, index, x):
    return pl.pallas_call(
        pick_kernel,
        grid_spec=pltpu.PrefetchScalarGridSpec(
            num_scalar_prefetch=2,
            grid=(1,),
            in_specs=[pl.BlockSpec(memory_space=pl.ANY)],
            out_specs=whole((HALF, B * K)),
            scratch_shapes=[
                pltpu.VMEM((HALF, CHIP), BF16),
                pltpu.VMEM((B * K // LB + 1, HALF, LB), F32),
                pltpu.SMEM((B * K + FLIGHT,), I32),
                pltpu.SemaphoreType.DMA((4,)),
            ],
        ),
        out_shape=jax.ShapeDtypeStruct((HALF, B * K), BF16),
        compiler_params=pltpu.CompilerParams(vmem_limit_bytes=PICK_LIMIT),
        cost_estimate=pl.CostEstimate(flops=0, bytes_accessed=2 * HALF * CHIP, transcendentals=0),
        name="pick",
    )(sp, index, x)


def places_kernel(
    sp_ref, seg_ref, place_ref, damp_ref, ext_ref, pick_ref, cols_ref, w_ref, count_ref
):
    first = sp_ref[1].astype(F32)
    last = first + (SEG_BLOCKS - 1)
    blocks = (seg_ref[...] * SEG_BLOCKS + (place_ref[...] >> 7)).astype(F32)
    reaches = ext_ref[...].astype(F32) + 1.0
    diagonal = iota((K, K), 0) == iota((K, K), 1)
    upper = ones_where(iota((K, K), 0) <= iota((K, K), 1))
    slots = iota((K, K), 0).astype(F32)
    most = I32(0)

    def column(mask, row):
        return jnp.sum(jnp.where(mask, row, 0.0), axis=1, keepdims=True)

    for b in range(B):
        block, reach, damping = blocks[b : b + 1], reaches[b : b + 1], damp_ref[b : b + 1, :]
        gap = jnp.maximum(jnp.maximum(first - block, block - last), 0.0)
        felt = (gap < reach).astype(F32)
        rank = dot(jnp.broadcast_to(felt, (8, K)).astype(BF16), upper)[0:1]
        chosen = jnp.where(felt > 0.0, rank - 1.0, -1.0) == slots
        most = jnp.maximum(most, jnp.sum(felt).astype(I32))
        pick_ref[b] = ones_where(chosen)
        cols_ref[b, 0] = jnp.broadcast_to(column(chosen, block), (K, LB))
        cols_ref[b, 1] = jnp.broadcast_to(jnp.maximum(column(chosen, reach), 1.0), (K, LB))
        cols_ref[b, 2] = jnp.broadcast_to(column(chosen, damping), (K, LB))
    count_ref[0] = most
    distance = jnp.abs(blocks[1:2] - column(diagonal, blocks[0:1]))
    reach = column(diagonal, reaches[0:1])
    damping = column(diagonal, damp_ref[0:1, :])
    w_ref[...] = damping * jnp.maximum(0.0, 1.0 - distance / reach)


def places(sp, segment, place, damping, extent):
    return pl.pallas_call(
        places_kernel,
        grid_spec=pltpu.PrefetchScalarGridSpec(
            num_scalar_prefetch=1,
            grid=(1,),
            in_specs=[whole((B, K))] * 4,
            out_specs=[
                whole((B, K, K)),
                whole((B, 3, K, LB)),
                whole((K, K)),
                pl.BlockSpec(memory_space=pltpu.SMEM),
            ],
        ),
        out_shape=[
            jax.ShapeDtypeStruct((B, K, K), BF16),
            jax.ShapeDtypeStruct((B, 3, K, LB), F32),
            jax.ShapeDtypeStruct((K, K), F32),
            jax.ShapeDtypeStruct((1,), I32),
        ],
        compiler_params=pltpu.CompilerParams(vmem_limit_bytes=VMEM_LIMIT),
        cost_estimate=pl.CostEstimate(
            flops=1_000_000, bytes_accessed=2_000_000, transcendentals=0
        ),
        name="places",
    )(sp, segment, place, damping, extent)


def observe_stats(prior, values, variances):
    centre = jnp.sum(prior, axis=0, keepdims=True) / MEMBERS
    anomaly = prior - centre
    prior_var = jnp.sum(anomaly * anomaly, axis=0, keepdims=True) / (MEMBERS - 1) + 1e-06
    post_var = 1.0 / (1.0 / prior_var + 1.0 / variances)
    post_mean = post_var * (centre / prior_var + values / variances)
    shrink = jnp.sqrt(post_var / prior_var)
    increment = (post_mean - centre + (shrink - 1.0) * anomaly).astype(BF16)
    scaled = (anomaly * (1.0 / ((MEMBERS - 1) * prior_var))).astype(BF16)
    left = jnp.sum(scaled.astype(F32), axis=0, keepdims=True) * (-1.0 / EXTRA)
    return increment, jnp.concatenate([scaled, jnp.broadcast_to(left, (EXTRA, K)).astype(BF16)], 0)


def with_extra(x):
    return jnp.concatenate([x, x[:EXTRA]], 0)


def stats_kernel(mine_ref, other_ref, val_ref, var_ref, pick_ref, w_ref, cov_ref, chg_ref):
    def prior(b):
        at = slice(b * K, (b + 1) * K)
        return jnp.concatenate([mine_ref[:, at].astype(F32), other_ref[:, at].astype(F32)], 0)

    increment0, scaled0 = observe_stats(prior(0), val_ref[0:1, :], var_ref[0:1, :])
    before = prior(1)
    eye = ones_where(iota((K, K), 0) == iota((K, K), 1))
    cov = dot(dot_nt(eye, scaled0).astype(BF16), with_extra(before.astype(BF16)))
    gain = (w_ref[...] * cov).astype(BF16)
    after = (before + dot(increment0, gain)).astype(BF16).astype(F32)
    increment1, scaled1 = observe_stats(after, val_ref[1:2, :], var_ref[1:2, :])
    for b, (increment, scaled) in enumerate(((increment0, scaled0), (increment1, scaled1))):
        cov_ref[b] = dot_nt(pick_ref[b], scaled).astype(BF16)
        chg_ref[b] = dot_nt(increment, pick_ref[b]).astype(BF16)


def stats(mine, other, readings, spread, picks, w):
    return pl.pallas_call(
        stats_kernel,
        grid=(1,),
        in_specs=[
            whole((HALF, B * K)),
            whole((HALF, B * K)),
            whole((B, K)),
            whole((B, K)),
            whole((B, K, K)),
            whole((K, K)),
        ],
        out_specs=[whole((B, K, DEPTH)), whole((B, MEMBERS, K))],
        out_shape=[
            jax.ShapeDtypeStruct((B, K, DEPTH), BF16),
            jax.ShapeDtypeStruct((B, MEMBERS, K), BF16),
        ],
        compiler_params=pltpu.CompilerParams(vmem_limit_bytes=VMEM_LIMIT),
        name="stats",
    )(mine, other, readings, spread, picks, w)


def moved(base, a):
    return pl.ds(pl.multiple_of(base + a.start, 256), 256)


def update_kernel(begin, sp_ref, count_ref, cov_ref, chg_ref, cols, mine_ref, other_ref, *rest):
    own_ref, away_ref = rest[-2:]
    step = pl.program_id(0) + begin
    there = sp_ref[0] * SD + step * CHUNK
    back = pl.program_id(0) * CHUNK
    first = sp_ref[1].astype(F32)

    def weights(b, kc):
        block = (first + (step * CHUNK_BLOCKS).astype(F32)) + iota((kc, LB), 1).astype(F32)
        distance = jnp.abs(block - cols[b, 0, :kc])
        return cols[b, 2, :kc] * jnp.maximum(0.0, 1.0 - distance / cols[b, 1, :kc])

    def advance(kc):
        w = [weights(b, kc) for b in range(B)]
        for start in range(0, CHUNK // 256, IN_FLIGHT[kc]):
            pairs = range(start, start + IN_FLIGHT[kc])
            at = [slice(p * 256, (p + 1) * 256) for p in pairs]
            wide = [
                jnp.concatenate(
                    [mine_ref[:, a].astype(F32), other_ref[:, moved(there, a)].astype(F32)], 0
                )
                for a in at
            ]
            for b in range(B):
                cov = [dot(cov_ref[b, :kc], with_extra(x.astype(BF16))) for x in wide]
                gain = [
                    jnp.concatenate(
                        [
                            c[:, h * LB : (h + 1) * LB]
                            * jnp.broadcast_to(w[b][:, 2 * p + h : 2 * p + h + 1], (kc, LB))
                            for h in range(2)
                        ],
                        1,
                    ).astype(BF16)
                    for p, c in zip(pairs, cov)
                ]
                wide = [x + dot(chg_ref[b, :, :kc], g) for x, g in zip(wide, gain)]
                if b == 0:
                    wide = [x.astype(BF16).astype(F32) for x in wide]
            for a, x in zip(at, wide):
                own_ref[:, a] = x[:HALF].astype(BF16)
                away_ref[:, moved(back, a)] = x[HALF:].astype(BF16)

    n = count_ref[0]

    @pl.when(n <= 32)
    def _():
        advance(32)

    @pl.when((n > 32) & (n <= 64))
    def _():
        advance(64)

    @pl.when((n > 64) & (n <= 128))
    def _():
        advance(128)

    @pl.when(n > 128)
    def _():
        advance(K)


def update(begin, steps, sp, count, cov, chg, cols, x, got, out):
    half = lambda i, s, c: (0, s[0] * STEPS + begin + i)
    in_specs = [pl.BlockSpec(memory_space=pltpu.VMEM)] * 3 + [
        pl.BlockSpec((HALF, CHUNK), half),
        pl.BlockSpec(memory_space=pltpu.VMEM),
    ]
    operands = [sp, count, cov, chg, cols, x, got]
    aliases = {}
    if out is not None:
        in_specs.append(pl.BlockSpec(memory_space=pl.ANY))
        operands.append(out)
        aliases = {len(operands) - 1: 0}
    return pl.pallas_call(
        lambda *refs: update_kernel(begin, *refs),
        grid_spec=pltpu.PrefetchScalarGridSpec(
            num_scalar_prefetch=2,
            grid=(steps,),
            in_specs=in_specs,
            out_specs=[
                pl.BlockSpec((HALF, CHUNK), half),
                pl.BlockSpec(memory_space=pltpu.VMEM),
            ],
        ),
        out_shape=[
            jax.ShapeDtypeStruct((HALF, CHIP), BF16),
            jax.ShapeDtypeStruct((HALF, steps * CHUNK), BF16),
        ],
        input_output_aliases=aliases,
        compiler_params=pltpu.CompilerParams(vmem_limit_bytes=VMEM_LIMIT),
        cost_estimate=pl.CostEstimate(
            flops=600_000_000 * steps,
            bytes_accessed=4 * MEMBERS * CHUNK * steps,
            transcendentals=0,
        ),
        name=f"update{begin}",
    )(*operands)


def fill(begins, sp, parts, out):
    def kernel(sp_ref, *refs):
        out_ref, sems = refs[-2:]
        base = (1 - sp_ref[0]) * SD
        copies = []
        for j, (begin, part) in enumerate(zip(begins, refs[: len(parts)])):
            width = part.shape[1] // PIECES
            for p in range(PIECES):
                start = pl.multiple_of(base + begin * CHUNK + p * width, 1024)
                to = out_ref.at[:, pl.ds(start, width)]
                piece = part.at[:, pl.ds(p * width, width)]
                copies.append(pltpu.make_async_copy(piece, to, sems.at[j * PIECES + p]))
        for copy in copies:
            copy.start()
        for copy in copies:
            copy.wait()

    return pl.pallas_call(
        kernel,
        grid_spec=pltpu.PrefetchScalarGridSpec(
            num_scalar_prefetch=1,
            grid=(1,),
            in_specs=[pl.BlockSpec(memory_space=pltpu.VMEM)] * len(parts)
            + [pl.BlockSpec(memory_space=pl.ANY)],
            out_specs=pl.BlockSpec(memory_space=pl.ANY),
            scratch_shapes=[pltpu.SemaphoreType.DMA((PIECES * len(parts),))],
        ),
        out_shape=jax.ShapeDtypeStruct((HALF, CHIP), BF16),
        input_output_aliases={1 + len(parts): 0},
        compiler_params=pltpu.CompilerParams(vmem_limit_bytes=VMEM_LIMIT),
        name=f"fill{begins[0]}",
    )(sp, *parts, out)


def sent(array, target):
    pairs = [(i, target(i)) for i in range(CHIPS)]
    return lax.ppermute(array, "state", [(i, j) for i, j in pairs if 0 <= j < CHIPS])


def along_row(array, by):
    return sent(array, lambda i: i // 4 * 4 + (i + by) % 4)


def across_rows(array, by):
    return sent(array, lambda i: i + 4 * by)


def swapped(array):
    return lax.ppermute(array, "mem", [(0, 1), (1, 0)])


def on_device(x, segment, place, readings, spread, damping, extent):
    core = lax.axis_index("mem")
    chip = lax.axis_index("state")
    sp = jnp.stack([core, (chip * 2 + core) * SEG_BLOCKS, chip]).astype(I32)

    picked = pick(sp, segment * SD + place, x)
    x, picked = lax.optimization_barrier((x, picked))
    two, one, three = (along_row(picked, by) for by in (2, 1, 3))
    got = swapped(x)
    picks, cols, w, count = places(sp, segment, place, damping, extent)
    near = picked + one + two + three
    near, picks, cols, w, count = lax.optimization_barrier((near, picks, cols, w, count))
    far = near + across_rows(near, 1) + across_rows(near, -1)
    cov, chg = stats(far, swapped(far), readings, spread, picks, w)
    out = None
    away = []
    begin = 0
    for steps in PARTS:
        out, part = update(begin, steps, sp, count, cov, chg, cols, x, got, out)
        away.append((begin, swapped(part)))
        begin += steps
    for some in (away[:-1], away[-1:]):
        out = fill([begin for begin, _ in some], sp, [part for _, part in some], out)
    return out


def solution(mesh):
    in_specs = (P("mem", "state"), P(), P(), P(), P(), P(), P())
    return jax.shard_map(
        on_device, mesh=mesh, in_specs=in_specs, out_specs=P("mem", "state"), check_vma=False
    )
```

```python
import jax
import jax.numpy as jnp
from jax import lax
from jax.experimental import pallas as pl
from jax.experimental.pallas import tpu as pltpu
from jax.sharding import PartitionSpec as P

MEMBERS = 80
HALF = 40
SD = 32768
K = 256
B = 2
LB = 128
CHIP = 2 * SD
CHIPS = 64
SEG_BLOCKS = SD // LB
CHUNK = 4096
STEPS = SD // CHUNK
CHUNK_BLOCKS = CHUNK // LB
PARTS = (6, 2)
IN_FLIGHT = {32: 16, 64: 16, 128: 8, K: 4}
PIECES = 4
FLIGHT = 16
EXTRA = 16
DEPTH = MEMBERS + EXTRA
F32 = jnp.float32
BF16 = jnp.bfloat16
I32 = jnp.int32
NT = (((1,), (1,)), ((), ()))
VMEM_LIMIT = 40 * 1024 * 1024
PICK_LIMIT = 40 * 1024 * 1024


def dot(a, b):
    return jnp.dot(a, b, preferred_element_type=F32)


def dot_nt(a, b):
    return lax.dot_general(a, b, NT, preferred_element_type=F32)


def iota(shape, dim):
    return lax.broadcasted_iota(I32, shape, dim)


def ones_where(mask):
    return mask.astype(F32).astype(BF16)


def whole(shape):
    return pl.BlockSpec(shape, lambda i, *s: (0,) * len(shape))


def pick_kernel(sp_ref, index_ref, x_ref, o_ref, xv, acc, owned, sems):
    parts = 4
    width = CHIP // parts
    copies = [
        pltpu.make_async_copy(
            x_ref.at[:, pl.ds(p * width, width)], xv.at[:, pl.ds(p * width, width)], sems.at[p]
        )
        for p in range(parts)
    ]
    for copy in copies:
        copy.start()
    acc[...] = jnp.zeros_like(acc)
    chip = sp_ref[2]
    n = I32(0)
    for b in range(B):

        def scan(k, n, b=b):
            owned[n] = b * K + k
            return n + ((index_ref[b, k] >> 16) == chip).astype(I32)

        n = lax.fori_loop(0, K, scan, n, unroll=16)
    for j in range(FLIGHT):
        owned[n + j] = B * K
    for copy in copies:
        copy.wait()
    lane = iota((HALF, LB), 1)

    def extract(i, _):
        for j in range(FLIGHT):
            k = owned[FLIGHT * i + j]
            b = jnp.minimum(k >> 8, B - 1)
            within = k & (K - 1)
            at = index_ref[b, within] & (CHIP - 1)
            start = pl.multiple_of((at >> 7) * LB, LB)
            tile = xv[:, pl.ds(start, LB)].astype(F32)
            turned = pltpu.roll(tile, (k - at) & (LB - 1), 1)
            pltpu.store(acc.at[k >> 7], turned, mask=lane == (k & (LB - 1)))
        return 0

    lax.fori_loop(0, (n + FLIGHT - 1) // FLIGHT, extract, 0)
    for g in range(B * K // LB):
        o_ref[:, g * LB : (g + 1) * LB] = acc[g].astype(BF16)


def pick(sp, index, x):
    return pl.pallas_call(
        pick_kernel,
        grid_spec=pltpu.PrefetchScalarGridSpec(
            num_scalar_prefetch=2,
            grid=(1,),
            in_specs=[pl.BlockSpec(memory_space=pl.ANY)],
            out_specs=whole((HALF, B * K)),
            scratch_shapes=[
                pltpu.VMEM((HALF, CHIP), BF16),
                pltpu.VMEM((B * K // LB + 1, HALF, LB), F32),
                pltpu.SMEM((B * K + FLIGHT,), I32),
                pltpu.SemaphoreType.DMA((4,)),
            ],
        ),
        out_shape=jax.ShapeDtypeStruct((HALF, B * K), BF16),
        compiler_params=pltpu.CompilerParams(vmem_limit_bytes=PICK_LIMIT),
        cost_estimate=pl.CostEstimate(flops=0, bytes_accessed=2 * HALF * CHIP, transcendentals=0),
        name="pick",
    )(sp, index, x)


def places_kernel(
    sp_ref, seg_ref, place_ref, damp_ref, ext_ref, pick_ref, cols_ref, w_ref, count_ref
):
    first = sp_ref[1].astype(F32)
    last = first + (SEG_BLOCKS - 1)
    blocks = (seg_ref[...] * SEG_BLOCKS + (place_ref[...] >> 7)).astype(F32)
    reaches = ext_ref[...].astype(F32) + 1.0
    diagonal = iota((K, K), 0) == iota((K, K), 1)
    upper = ones_where(iota((K, K), 0) <= iota((K, K), 1))
    slots = iota((K, K), 0).astype(F32)
    most = I32(0)

    def column(mask, row):
        return jnp.sum(jnp.where(mask, row, 0.0), axis=1, keepdims=True)

    for b in range(B):
        block, reach, damping = blocks[b : b + 1], reaches[b : b + 1], damp_ref[b : b + 1, :]
        gap = jnp.maximum(jnp.maximum(first - block, block - last), 0.0)
        felt = (gap < reach).astype(F32)
        rank = dot(jnp.broadcast_to(felt, (8, K)).astype(BF16), upper)[0:1]
        chosen = jnp.where(felt > 0.0, rank - 1.0, -1.0) == slots
        most = jnp.maximum(most, jnp.sum(felt).astype(I32))
        pick_ref[b] = ones_where(chosen)
        cols_ref[b, 0] = jnp.broadcast_to(column(chosen, block), (K, LB))
        cols_ref[b, 1] = jnp.broadcast_to(jnp.maximum(column(chosen, reach), 1.0), (K, LB))
        cols_ref[b, 2] = jnp.broadcast_to(column(chosen, damping), (K, LB))
    count_ref[0] = most
    distance = jnp.abs(blocks[1:2] - column(diagonal, blocks[0:1]))
    reach = column(diagonal, reaches[0:1])
    damping = column(diagonal, damp_ref[0:1, :])
    w_ref[...] = damping * jnp.maximum(0.0, 1.0 - distance / reach)


def places(sp, segment, place, damping, extent):
    return pl.pallas_call(
        places_kernel,
        grid_spec=pltpu.PrefetchScalarGridSpec(
            num_scalar_prefetch=1,
            grid=(1,),
            in_specs=[whole((B, K))] * 4,
            out_specs=[
                whole((B, K, K)),
                whole((B, 3, K, LB)),
                whole((K, K)),
                pl.BlockSpec(memory_space=pltpu.SMEM),
            ],
        ),
        out_shape=[
            jax.ShapeDtypeStruct((B, K, K), BF16),
            jax.ShapeDtypeStruct((B, 3, K, LB), F32),
            jax.ShapeDtypeStruct((K, K), F32),
            jax.ShapeDtypeStruct((1,), I32),
        ],
        compiler_params=pltpu.CompilerParams(vmem_limit_bytes=VMEM_LIMIT),
        cost_estimate=pl.CostEstimate(
            flops=1_000_000, bytes_accessed=2_000_000, transcendentals=0
        ),
        name="places",
    )(sp, segment, place, damping, extent)


def observe_stats(prior, values, variances):
    centre = jnp.sum(prior, axis=0, keepdims=True) / MEMBERS
    anomaly = prior - centre
    prior_var = jnp.sum(anomaly * anomaly, axis=0, keepdims=True) / (MEMBERS - 1) + 1e-06
    post_var = 1.0 / (1.0 / prior_var + 1.0 / variances)
    post_mean = post_var * (centre / prior_var + values / variances)
    shrink = jnp.sqrt(post_var / prior_var)
    increment = (post_mean - centre + (shrink - 1.0) * anomaly).astype(BF16)
    scaled = (anomaly * (1.0 / ((MEMBERS - 1) * prior_var))).astype(BF16)
    left = jnp.sum(scaled.astype(F32), axis=0, keepdims=True) * (-1.0 / EXTRA)
    return increment, jnp.concatenate([scaled, jnp.broadcast_to(left, (EXTRA, K)).astype(BF16)], 0)


def with_extra(x):
    return jnp.concatenate([x, x[:EXTRA]], 0)


def stats_kernel(mine_ref, other_ref, val_ref, var_ref, pick_ref, w_ref, cov_ref, chg_ref):
    def prior(b):
        at = slice(b * K, (b + 1) * K)
        return jnp.concatenate([mine_ref[:, at].astype(F32), other_ref[:, at].astype(F32)], 0)

    increment0, scaled0 = observe_stats(prior(0), val_ref[0:1, :], var_ref[0:1, :])
    before = prior(1)
    eye = ones_where(iota((K, K), 0) == iota((K, K), 1))
    cov = dot(dot_nt(eye, scaled0).astype(BF16), with_extra(before.astype(BF16)))
    gain = (w_ref[...] * cov).astype(BF16)
    after = (before + dot(increment0, gain)).astype(BF16).astype(F32)
    increment1, scaled1 = observe_stats(after, val_ref[1:2, :], var_ref[1:2, :])
    for b, (increment, scaled) in enumerate(((increment0, scaled0), (increment1, scaled1))):
        cov_ref[b] = dot_nt(pick_ref[b], scaled).astype(BF16)
        chg_ref[b] = dot_nt(increment, pick_ref[b]).astype(BF16)


def stats(mine, other, readings, spread, picks, w):
    return pl.pallas_call(
        stats_kernel,
        grid=(1,),
        in_specs=[
            whole((HALF, B * K)),
            whole((HALF, B * K)),
            whole((B, K)),
            whole((B, K)),
            whole((B, K, K)),
            whole((K, K)),
        ],
        out_specs=[whole((B, K, DEPTH)), whole((B, MEMBERS, K))],
        out_shape=[
            jax.ShapeDtypeStruct((B, K, DEPTH), BF16),
            jax.ShapeDtypeStruct((B, MEMBERS, K), BF16),
        ],
        compiler_params=pltpu.CompilerParams(vmem_limit_bytes=VMEM_LIMIT),
        name="stats",
    )(mine, other, readings, spread, picks, w)


def moved(base, a):
    return pl.ds(pl.multiple_of(base + a, 256), 256)


def update_kernel(begin, sp_ref, count_ref, cov_ref, chg_ref, cols, mine_ref, other_ref, *rest):
    own_ref, away_ref = rest[-2:]
    step = pl.program_id(0) + begin
    there = sp_ref[0] * SD + step * CHUNK
    back = pl.program_id(0) * CHUNK
    first = sp_ref[1].astype(F32)

    def weights(b, kc, start):
        block = (first + (step * CHUNK_BLOCKS + start).astype(F32)) + iota((kc, LB), 1).astype(F32)
        distance = jnp.abs(block - cols[b, 0, :kc])
        return cols[b, 2, :kc] * jnp.maximum(0.0, 1.0 - distance / cols[b, 1, :kc])

    def advance_pairs(kc, start):
        pairs = range(IN_FLIGHT[kc])
        at = [pl.multiple_of((start + p) * 256, 256) for p in pairs]
        w = [weights(b, kc, 2 * start) for b in range(B)]
        wide = [
            jnp.concatenate(
                [
                    mine_ref[:, pl.ds(a, 256)].astype(F32),
                    other_ref[:, moved(there, a)].astype(F32),
                ],
                0,
            )
            for a in at
        ]
        for b in range(B):
            cov = [dot(cov_ref[b, :kc], with_extra(x.astype(BF16))) for x in wide]
            gain = [
                jnp.concatenate(
                    [
                        c[:, h * LB : (h + 1) * LB]
                        * jnp.broadcast_to(w[b][:, 2 * p + h : 2 * p + h + 1], (kc, LB))
                        for h in range(2)
                    ],
                    1,
                ).astype(BF16)
                for p, c in zip(pairs, cov)
            ]
            wide = [x + dot(chg_ref[b, :, :kc], g) for x, g in zip(wide, gain)]
            if b == 0:
                wide = [x.astype(BF16).astype(F32) for x in wide]
        for a, x in zip(at, wide):
            own_ref[:, pl.ds(a, 256)] = x[:HALF].astype(BF16)
            away_ref[:, moved(back, a)] = x[HALF:].astype(BF16)

    def advance(kc):
        rounds = CHUNK // 256 // IN_FLIGHT[kc]

        def body(i, _):
            advance_pairs(kc, i * IN_FLIGHT[kc])
            return 0

        lax.fori_loop(0, rounds, body, 0)

    n = count_ref[0]

    @pl.when(n <= 32)
    def _():
        advance(32)

    @pl.when((n > 32) & (n <= 64))
    def _():
        advance(64)

    @pl.when((n > 64) & (n <= 128))
    def _():
        advance(128)

    @pl.when(n > 128)
    def _():
        advance(K)


def update(begin, steps, sp, count, cov, chg, cols, x, got, out):
    half = lambda i, s, c: (0, s[0] * STEPS + begin + i)
    in_specs = [pl.BlockSpec(memory_space=pltpu.VMEM)] * 3 + [
        pl.BlockSpec((HALF, CHUNK), half),
        pl.BlockSpec(memory_space=pltpu.VMEM),
    ]
    operands = [sp, count, cov, chg, cols, x, got]
    aliases = {}
    if out is not None:
        in_specs.append(pl.BlockSpec(memory_space=pl.ANY))
        operands.append(out)
        aliases = {len(operands) - 1: 0}
    return pl.pallas_call(
        lambda *refs: update_kernel(begin, *refs),
        grid_spec=pltpu.PrefetchScalarGridSpec(
            num_scalar_prefetch=2,
            grid=(steps,),
            in_specs=in_specs,
            out_specs=[
                pl.BlockSpec((HALF, CHUNK), half),
                pl.BlockSpec(memory_space=pltpu.VMEM),
            ],
        ),
        out_shape=[
            jax.ShapeDtypeStruct((HALF, CHIP), BF16),
            jax.ShapeDtypeStruct((HALF, steps * CHUNK), BF16),
        ],
        input_output_aliases=aliases,
        compiler_params=pltpu.CompilerParams(vmem_limit_bytes=VMEM_LIMIT),
        cost_estimate=pl.CostEstimate(
            flops=600_000_000 * steps,
            bytes_accessed=4 * MEMBERS * CHUNK * steps,
            transcendentals=0,
        ),
        name=f"update{begin}",
    )(*operands)


def fill(begins, parts, out):
    def kernel(*refs):
        out_ref, sems = refs[-2:]
        base = (1 - lax.axis_index("mem")) * SD
        copies = []
        for j, (begin, part) in enumerate(zip(begins, refs[: len(parts)])):
            width = part.shape[1] // PIECES
            for p in range(PIECES):
                start = pl.multiple_of(base + begin * CHUNK + p * width, 1024)
                to = out_ref.at[:, pl.ds(start, width)]
                piece = part.at[:, pl.ds(p * width, width)]
                copies.append(pltpu.make_async_copy(piece, to, sems.at[j * PIECES + p]))
        for copy in copies:
            copy.start()
        for copy in copies:
            copy.wait()

    return pl.pallas_call(
        kernel,
        in_specs=[pl.BlockSpec(memory_space=pltpu.VMEM)] * len(parts)
        + [pl.BlockSpec(memory_space=pl.ANY)],
        out_specs=pl.BlockSpec(memory_space=pl.ANY),
        scratch_shapes=[pltpu.SemaphoreType.DMA((PIECES * len(parts),))],
        out_shape=jax.ShapeDtypeStruct((HALF, CHIP), BF16),
        input_output_aliases={len(parts): 0},
        compiler_params=pltpu.CompilerParams(vmem_limit_bytes=VMEM_LIMIT),
        name=f"fill{begins[0]}",
    )(*parts, out)


def sent(array, target):
    pairs = [(i, target(i)) for i in range(CHIPS)]
    return lax.ppermute(array, "state", [(i, j) for i, j in pairs if 0 <= j < CHIPS])


def along_row(array, bits):
    return sent(array, lambda i: i ^ bits)


def across_rows(array, first):
    def partner(i):
        row = i // 4
        return i + 4 if row % 2 == first else i - 4

    return sent(array, partner)


def swapped(array):
    return lax.ppermute(array, "mem", [(0, 1), (1, 0)])


def on_device(x, segment, place, readings, spread, damping, extent):
    core = lax.axis_index("mem")
    chip = lax.axis_index("state")
    sp = jnp.stack([core, (chip * 2 + core) * SEG_BLOCKS, chip]).astype(I32)

    picked = pick(sp, segment * SD + place, x)
    x, picked = lax.optimization_barrier((x, picked))
    two, one, three = (along_row(picked, bits) for bits in (2, 1, 3))
    got = swapped(x)
    picks, cols, w, count = places(sp, segment, place, damping, extent)
    near = picked + one + two + three
    near, picks, cols, w, count = lax.optimization_barrier((near, picks, cols, w, count))
    far = near + across_rows(near, 1) + across_rows(near, 0)
    cov, chg = stats(far, swapped(far), readings, spread, picks, w)
    out = None
    away = []
    begin = 0
    for steps in PARTS:
        out, part = update(begin, steps, sp, count, cov, chg, cols, x, got, out)
        away.append((begin, swapped(part)))
        begin += steps
    for some in (away[:-1], away[-1:]):
        out = fill([begin for begin, _ in some], [part for _, part in some], out)
    return out


def solution(mesh):
    in_specs = (P("mem", "state"), P(), P(), P(), P(), P(), P())
    return jax.shard_map(
        on_device, mesh=mesh, in_specs=in_specs, out_specs=P("mem", "state"), check_vma=False
    )
```

```python
import jax
import jax.numpy as jnp
from jax import lax
from jax.experimental import pallas as pl
from jax.experimental.pallas import tpu as pltpu
from jax.sharding import PartitionSpec as P

MEMBERS = 80
HALF = 40
SD = 32768
K = 256
B = 2
LB = 128
CHIP = 2 * SD
CHIPS = 64
SEG_BLOCKS = SD // LB
CHUNK = 8192
STEPS = SD // CHUNK
CHUNK_BLOCKS = CHUNK // LB
PARTS = (3, 1)
IN_FLIGHT = {32: 32, 64: 32, 128: 8, K: 4}
PIECES = 4
FLIGHT = 16
EXTRA = 16
DEPTH = MEMBERS + EXTRA
F32 = jnp.float32
BF16 = jnp.bfloat16
I32 = jnp.int32
NT = (((1,), (1,)), ((), ()))
VMEM_LIMIT = 40 * 1024 * 1024
PICK_LIMIT = 40 * 1024 * 1024


def dot(a, b):
    return jnp.dot(a, b, preferred_element_type=F32)


def dot_nt(a, b):
    return lax.dot_general(a, b, NT, preferred_element_type=F32)


def iota(shape, dim):
    return lax.broadcasted_iota(I32, shape, dim)


def ones_where(mask):
    return mask.astype(F32).astype(BF16)


def whole(shape):
    return pl.BlockSpec(shape, lambda i, *s: (0,) * len(shape))


def pick_kernel(sp_ref, index_ref, x_ref, o_ref, xv, acc, owned, sems):
    parts = 4
    width = CHIP // parts
    copies = [
        pltpu.make_async_copy(
            x_ref.at[:, pl.ds(p * width, width)], xv.at[:, pl.ds(p * width, width)], sems.at[p]
        )
        for p in range(parts)
    ]
    for copy in copies:
        copy.start()
    acc[...] = jnp.zeros_like(acc)
    chip = sp_ref[2]
    n = I32(0)
    for b in range(B):

        def scan(k, n, b=b):
            owned[n] = b * K + k
            return n + ((index_ref[b, k] >> 16) == chip).astype(I32)

        n = lax.fori_loop(0, K, scan, n, unroll=16)
    for j in range(FLIGHT):
        owned[n + j] = B * K
    for copy in copies:
        copy.wait()
    lane = iota((HALF, LB), 1)

    def extract(i, _):
        for j in range(FLIGHT):
            k = owned[FLIGHT * i + j]
            b = jnp.minimum(k >> 8, B - 1)
            within = k & (K - 1)
            at = index_ref[b, within] & (CHIP - 1)
            start = pl.multiple_of((at >> 7) * LB, LB)
            tile = xv[:, pl.ds(start, LB)].astype(F32)
            turned = pltpu.roll(tile, (k - at) & (LB - 1), 1)
            pltpu.store(acc.at[k >> 7], turned, mask=lane == (k & (LB - 1)))
        return 0

    lax.fori_loop(0, (n + FLIGHT - 1) // FLIGHT, extract, 0)
    for g in range(B * K // LB):
        o_ref[:, g * LB : (g + 1) * LB] = acc[g].astype(BF16)


def pick(sp, index, x):
    return pl.pallas_call(
        pick_kernel,
        grid_spec=pltpu.PrefetchScalarGridSpec(
            num_scalar_prefetch=2,
            grid=(1,),
            in_specs=[pl.BlockSpec(memory_space=pl.ANY)],
            out_specs=whole((HALF, B * K)),
            scratch_shapes=[
                pltpu.VMEM((HALF, CHIP), BF16),
                pltpu.VMEM((B * K // LB + 1, HALF, LB), F32),
                pltpu.SMEM((B * K + FLIGHT,), I32),
                pltpu.SemaphoreType.DMA((4,)),
            ],
        ),
        out_shape=jax.ShapeDtypeStruct((HALF, B * K), BF16),
        compiler_params=pltpu.CompilerParams(vmem_limit_bytes=PICK_LIMIT),
        cost_estimate=pl.CostEstimate(flops=0, bytes_accessed=2 * HALF * CHIP, transcendentals=0),
        name="pick",
    )(sp, index, x)


def places_kernel(
    sp_ref, seg_ref, place_ref, damp_ref, ext_ref, pick_ref, cols_ref, w_ref, count_ref
):
    first = sp_ref[1].astype(F32)
    last = first + (SEG_BLOCKS - 1)
    blocks = (seg_ref[...] * SEG_BLOCKS + (place_ref[...] >> 7)).astype(F32)
    reaches = ext_ref[...].astype(F32) + 1.0
    diagonal = iota((K, K), 0) == iota((K, K), 1)
    upper = ones_where(iota((K, K), 0) <= iota((K, K), 1))
    slots = iota((K, K), 0).astype(F32)
    most = I32(0)

    def column(mask, row):
        return jnp.sum(jnp.where(mask, row, 0.0), axis=1, keepdims=True)

    for b in range(B):
        block, reach, damping = blocks[b : b + 1], reaches[b : b + 1], damp_ref[b : b + 1, :]
        gap = jnp.maximum(jnp.maximum(first - block, block - last), 0.0)
        felt = (gap < reach).astype(F32)
        rank = dot(jnp.broadcast_to(felt, (8, K)).astype(BF16), upper)[0:1]
        chosen = jnp.where(felt > 0.0, rank - 1.0, -1.0) == slots
        most = jnp.maximum(most, jnp.sum(felt).astype(I32))
        pick_ref[b] = ones_where(chosen)
        cols_ref[b, 0] = jnp.broadcast_to(column(chosen, block), (K, LB))
        cols_ref[b, 1] = jnp.broadcast_to(jnp.maximum(column(chosen, reach), 1.0), (K, LB))
        cols_ref[b, 2] = jnp.broadcast_to(column(chosen, damping), (K, LB))
    count_ref[0] = most
    distance = jnp.abs(blocks[1:2] - column(diagonal, blocks[0:1]))
    reach = column(diagonal, reaches[0:1])
    damping = column(diagonal, damp_ref[0:1, :])
    w_ref[...] = damping * jnp.maximum(0.0, 1.0 - distance / reach)


def places(sp, segment, place, damping, extent):
    return pl.pallas_call(
        places_kernel,
        grid_spec=pltpu.PrefetchScalarGridSpec(
            num_scalar_prefetch=1,
            grid=(1,),
            in_specs=[whole((B, K))] * 4,
            out_specs=[
                whole((B, K, K)),
                whole((B, 3, K, LB)),
                whole((K, K)),
                pl.BlockSpec(memory_space=pltpu.SMEM),
            ],
        ),
        out_shape=[
            jax.ShapeDtypeStruct((B, K, K), BF16),
            jax.ShapeDtypeStruct((B, 3, K, LB), F32),
            jax.ShapeDtypeStruct((K, K), F32),
            jax.ShapeDtypeStruct((1,), I32),
        ],
        compiler_params=pltpu.CompilerParams(vmem_limit_bytes=VMEM_LIMIT),
        cost_estimate=pl.CostEstimate(
            flops=1_000_000, bytes_accessed=2_000_000, transcendentals=0
        ),
        name="places",
    )(sp, segment, place, damping, extent)


def observe_stats(prior, values, variances):
    centre = jnp.sum(prior, axis=0, keepdims=True) / MEMBERS
    anomaly = prior - centre
    prior_var = jnp.sum(anomaly * anomaly, axis=0, keepdims=True) / (MEMBERS - 1) + 1e-06
    post_var = 1.0 / (1.0 / prior_var + 1.0 / variances)
    post_mean = post_var * (centre / prior_var + values / variances)
    shrink = jnp.sqrt(post_var / prior_var)
    increment = (post_mean - centre + (shrink - 1.0) * anomaly).astype(BF16)
    scaled = (anomaly * (1.0 / ((MEMBERS - 1) * prior_var))).astype(BF16)
    left = jnp.sum(scaled.astype(F32), axis=0, keepdims=True) * (-1.0 / EXTRA)
    return increment, jnp.concatenate([scaled, jnp.broadcast_to(left, (EXTRA, K)).astype(BF16)], 0)


def with_extra(x):
    return jnp.concatenate([x, x[:EXTRA]], 0)


def stats_kernel(mine_ref, other_ref, val_ref, var_ref, pick_ref, w_ref, cov_ref, chg_ref):
    def prior(b):
        at = slice(b * K, (b + 1) * K)
        return jnp.concatenate([mine_ref[:, at].astype(F32), other_ref[:, at].astype(F32)], 0)

    increment0, scaled0 = observe_stats(prior(0), val_ref[0:1, :], var_ref[0:1, :])
    before = prior(1)
    eye = ones_where(iota((K, K), 0) == iota((K, K), 1))
    cov = dot(dot_nt(eye, scaled0).astype(BF16), with_extra(before.astype(BF16)))
    gain = (w_ref[...] * cov).astype(BF16)
    after = (before + dot(increment0, gain)).astype(BF16).astype(F32)
    increment1, scaled1 = observe_stats(after, val_ref[1:2, :], var_ref[1:2, :])
    for b, (increment, scaled) in enumerate(((increment0, scaled0), (increment1, scaled1))):
        cov_ref[b] = dot_nt(pick_ref[b], scaled).astype(BF16)
        chg_ref[b] = dot_nt(increment, pick_ref[b]).astype(BF16)


def stats(mine, other, readings, spread, picks, w):
    return pl.pallas_call(
        stats_kernel,
        grid=(1,),
        in_specs=[
            whole((HALF, B * K)),
            whole((HALF, B * K)),
            whole((B, K)),
            whole((B, K)),
            whole((B, K, K)),
            whole((K, K)),
        ],
        out_specs=[whole((B, K, DEPTH)), whole((B, MEMBERS, K))],
        out_shape=[
            jax.ShapeDtypeStruct((B, K, DEPTH), BF16),
            jax.ShapeDtypeStruct((B, MEMBERS, K), BF16),
        ],
        compiler_params=pltpu.CompilerParams(vmem_limit_bytes=VMEM_LIMIT),
        name="stats",
    )(mine, other, readings, spread, picks, w)


def moved(base, a):
    return pl.ds(pl.multiple_of(base + a, 256), 256)


def update_kernel(begin, sp_ref, count_ref, cov_ref, chg_ref, cols, mine_ref, other_ref, *rest):
    own_ref, away_ref = rest[-2:]
    step = pl.program_id(0) + begin
    there = sp_ref[0] * SD + step * CHUNK
    back = pl.program_id(0) * CHUNK
    first = sp_ref[1].astype(F32)

    def weights(b, kc, start):
        block = (first + (step * CHUNK_BLOCKS + start).astype(F32)) + iota((kc, LB), 1).astype(F32)
        distance = jnp.abs(block - cols[b, 0, :kc])
        return cols[b, 2, :kc] * jnp.maximum(0.0, 1.0 - distance / cols[b, 1, :kc])

    def advance_pairs(kc, start):
        pairs = range(IN_FLIGHT[kc])
        at = [pl.multiple_of((start + p) * 256, 256) for p in pairs]
        w = [weights(b, kc, 2 * start) for b in range(B)]
        wide = [
            jnp.concatenate(
                [
                    mine_ref[:, pl.ds(a, 256)].astype(F32),
                    other_ref[:, moved(there, a)].astype(F32),
                ],
                0,
            )
            for a in at
        ]
        for b in range(B):
            cov = [dot(cov_ref[b, :kc], with_extra(x.astype(BF16))) for x in wide]
            gain = [
                jnp.concatenate(
                    [
                        c[:, h * LB : (h + 1) * LB]
                        * jnp.broadcast_to(w[b][:, 2 * p + h : 2 * p + h + 1], (kc, LB))
                        for h in range(2)
                    ],
                    1,
                ).astype(BF16)
                for p, c in zip(pairs, cov)
            ]
            wide = [x + dot(chg_ref[b, :, :kc], g) for x, g in zip(wide, gain)]
            if b == 0:
                wide = [x.astype(BF16).astype(F32) for x in wide]
        for a, x in zip(at, wide):
            own_ref[:, pl.ds(a, 256)] = x[:HALF].astype(BF16)
            away_ref[:, moved(back, a)] = x[HALF:].astype(BF16)

    def advance(kc):
        rounds = CHUNK // 256 // IN_FLIGHT[kc]

        def body(i, _):
            advance_pairs(kc, i * IN_FLIGHT[kc])
            return 0

        lax.fori_loop(0, rounds, body, 0)

    n = count_ref[0]

    @pl.when(n <= 32)
    def _():
        advance(32)

    @pl.when((n > 32) & (n <= 64))
    def _():
        advance(64)

    @pl.when((n > 64) & (n <= 128))
    def _():
        advance(128)

    @pl.when(n > 128)
    def _():
        advance(K)


def update(begin, steps, sp, count, cov, chg, cols, x, got, out):
    half = lambda i, s, c: (0, s[0] * STEPS + begin + i)
    in_specs = [pl.BlockSpec(memory_space=pltpu.VMEM)] * 3 + [
        pl.BlockSpec((HALF, CHUNK), half),
        pl.BlockSpec(memory_space=pltpu.VMEM),
    ]
    operands = [sp, count, cov, chg, cols, x, got]
    aliases = {}
    if out is not None:
        in_specs.append(pl.BlockSpec(memory_space=pl.ANY))
        operands.append(out)
        aliases = {len(operands) - 1: 0}
    return pl.pallas_call(
        lambda *refs: update_kernel(begin, *refs),
        grid_spec=pltpu.PrefetchScalarGridSpec(
            num_scalar_prefetch=2,
            grid=(steps,),
            in_specs=in_specs,
            out_specs=[
                pl.BlockSpec((HALF, CHUNK), half),
                pl.BlockSpec(memory_space=pltpu.VMEM),
            ],
        ),
        out_shape=[
            jax.ShapeDtypeStruct((HALF, CHIP), BF16),
            jax.ShapeDtypeStruct((HALF, steps * CHUNK), BF16),
        ],
        input_output_aliases=aliases,
        compiler_params=pltpu.CompilerParams(vmem_limit_bytes=VMEM_LIMIT),
        cost_estimate=pl.CostEstimate(
            flops=600_000_000 * steps,
            bytes_accessed=4 * MEMBERS * CHUNK * steps,
            transcendentals=0,
        ),
        name=f"update{begin}",
    )(*operands)


def fill(begins, parts, out):
    def kernel(*refs):
        out_ref, sems = refs[-2:]
        base = (1 - lax.axis_index("mem")) * SD
        copies = []
        for j, (begin, part) in enumerate(zip(begins, refs[: len(parts)])):
            width = part.shape[1] // PIECES
            for p in range(PIECES):
                start = pl.multiple_of(base + begin * CHUNK + p * width, 1024)
                to = out_ref.at[:, pl.ds(start, width)]
                piece = part.at[:, pl.ds(p * width, width)]
                copies.append(pltpu.make_async_copy(piece, to, sems.at[j * PIECES + p]))
        for copy in copies:
            copy.start()
        for copy in copies:
            copy.wait()

    return pl.pallas_call(
        kernel,
        in_specs=[pl.BlockSpec(memory_space=pltpu.VMEM)] * len(parts)
        + [pl.BlockSpec(memory_space=pl.ANY)],
        out_specs=pl.BlockSpec(memory_space=pl.ANY),
        scratch_shapes=[pltpu.SemaphoreType.DMA((PIECES * len(parts),))],
        out_shape=jax.ShapeDtypeStruct((HALF, CHIP), BF16),
        input_output_aliases={len(parts): 0},
        compiler_params=pltpu.CompilerParams(vmem_limit_bytes=VMEM_LIMIT),
        name=f"fill{begins[0]}",
    )(*parts, out)


def sent(array, target):
    pairs = [(i, target(i)) for i in range(CHIPS)]
    return lax.ppermute(array, "state", [(i, j) for i, j in pairs if 0 <= j < CHIPS])


def along_row(array, bits):
    return sent(array, lambda i: i ^ bits)


def across_rows(array, first):
    def partner(i):
        row = i // 4
        return i + 4 if row % 2 == first else i - 4

    return sent(array, partner)


def swapped(array):
    return lax.ppermute(array, "mem", [(0, 1), (1, 0)])


def on_device(x, segment, place, readings, spread, damping, extent):
    core = lax.axis_index("mem")
    chip = lax.axis_index("state")
    sp = jnp.stack([core, (chip * 2 + core) * SEG_BLOCKS, chip]).astype(I32)

    picked = pick(sp, segment * SD + place, x)
    x, picked = lax.optimization_barrier((x, picked))
    two, one, three = (along_row(picked, bits) for bits in (2, 1, 3))
    got = swapped(x)
    picks, cols, w, count = places(sp, segment, place, damping, extent)
    near = picked + one + two + three
    near, picks, cols, w, count = lax.optimization_barrier((near, picks, cols, w, count))
    far = near + across_rows(near, 0) + across_rows(near, 1)
    cov, chg = stats(far, swapped(far), readings, spread, picks, w)
    out = None
    away = []
    begin = 0
    for steps in PARTS:
        out, part = update(begin, steps, sp, count, cov, chg, cols, x, got, out)
        away.append((begin, swapped(part)))
        begin += steps
    for some in (away[:-1], away[-1:]):
        out = fill([begin for begin, _ in some], [part for _, part in some], out)
    return out


def solution(mesh):
    in_specs = (P("mem", "state"), P(), P(), P(), P(), P(), P())
    return jax.shard_map(
        on_device, mesh=mesh, in_specs=in_specs, out_specs=P("mem", "state"), check_vma=False
    )
```

```python
import jax
import jax.numpy as jnp
from jax import lax
from jax.experimental import pallas as pl
from jax.experimental.pallas import tpu as pltpu
from jax.sharding import PartitionSpec as P

MEMBERS = 80
HALF = 40
SD = 32768
K = 256
B = 2
LB = 128
CHIP = 2 * SD
CHIPS = 64
SEG_BLOCKS = SD // LB
CHUNK = 8192
STEPS = SD // CHUNK
CHUNK_BLOCKS = CHUNK // LB
PARTS = (3, 1)
IN_FLIGHT = {32: 32, 64: 32, 128: 8, K: 4}
PIECES = 4
FLIGHT = 16
EXTRA = 16
DEPTH = MEMBERS + EXTRA
F32 = jnp.float32
BF16 = jnp.bfloat16
I32 = jnp.int32
NT = (((1,), (1,)), ((), ()))
VMEM_LIMIT = 40 * 1024 * 1024
PICK_LIMIT = 40 * 1024 * 1024


def dot(a, b):
    return jnp.dot(a, b, preferred_element_type=F32)


def dot_nt(a, b):
    return lax.dot_general(a, b, NT, preferred_element_type=F32)


def iota(shape, dim):
    return lax.broadcasted_iota(I32, shape, dim)


def ones_where(mask):
    return mask.astype(F32).astype(BF16)


def whole(shape):
    return pl.BlockSpec(shape, lambda i, *s: (0,) * len(shape))


def pick_kernel(sp_ref, index_ref, x_ref, o_ref, xv, acc, owned, sems):
    parts = 4
    width = CHIP // parts
    copies = [
        pltpu.make_async_copy(
            x_ref.at[:, pl.ds(p * width, width)], xv.at[:, pl.ds(p * width, width)], sems.at[p]
        )
        for p in range(parts)
    ]
    for copy in copies:
        copy.start()
    acc[...] = jnp.zeros_like(acc)
    chip = sp_ref[2]
    n = I32(0)
    for b in range(B):

        def scan(k, n, b=b):
            owned[n] = b * K + k
            return n + ((index_ref[b, k] >> 16) == chip).astype(I32)

        n = lax.fori_loop(0, K, scan, n, unroll=16)
    for j in range(FLIGHT):
        owned[n + j] = B * K
    for copy in copies:
        copy.wait()
    lane = iota((HALF, LB), 1)

    def extract(i, _):
        for j in range(FLIGHT):
            k = owned[FLIGHT * i + j]
            b = jnp.minimum(k >> 8, B - 1)
            within = k & (K - 1)
            at = index_ref[b, within] & (CHIP - 1)
            start = pl.multiple_of((at >> 7) * LB, LB)
            tile = xv[:, pl.ds(start, LB)].astype(F32)
            turned = pltpu.roll(tile, (k - at) & (LB - 1), 1)
            pltpu.store(acc.at[k >> 7], turned, mask=lane == (k & (LB - 1)))
        return 0

    lax.fori_loop(0, (n + FLIGHT - 1) // FLIGHT, extract, 0)
    for g in range(B * K // LB):
        o_ref[:, g * LB : (g + 1) * LB] = acc[g].astype(BF16)


def pick(sp, index, x):
    return pl.pallas_call(
        pick_kernel,
        grid_spec=pltpu.PrefetchScalarGridSpec(
            num_scalar_prefetch=2,
            grid=(1,),
            in_specs=[pl.BlockSpec(memory_space=pl.ANY)],
            out_specs=whole((HALF, B * K)),
            scratch_shapes=[
                pltpu.VMEM((HALF, CHIP), BF16),
                pltpu.VMEM((B * K // LB + 1, HALF, LB), F32),
                pltpu.SMEM((B * K + FLIGHT,), I32),
                pltpu.SemaphoreType.DMA((4,)),
            ],
        ),
        out_shape=jax.ShapeDtypeStruct((HALF, B * K), BF16),
        compiler_params=pltpu.CompilerParams(vmem_limit_bytes=PICK_LIMIT),
        cost_estimate=pl.CostEstimate(flops=0, bytes_accessed=2 * HALF * CHIP, transcendentals=0),
        name="pick",
    )(sp, index, x)


def places_kernel(
    sp_ref, seg_ref, place_ref, damp_ref, ext_ref, pick_ref, cols_ref, w_ref, count_ref
):
    first = sp_ref[1].astype(F32)
    last = first + (SEG_BLOCKS - 1)
    blocks = (seg_ref[...] * SEG_BLOCKS + (place_ref[...] >> 7)).astype(F32)
    reaches = ext_ref[...].astype(F32) + 1.0
    diagonal = iota((K, K), 0) == iota((K, K), 1)
    upper = ones_where(iota((K, K), 0) <= iota((K, K), 1))
    slots = iota((K, K), 0).astype(F32)
    most = I32(0)

    def column(mask, row):
        return jnp.sum(jnp.where(mask, row, 0.0), axis=1, keepdims=True)

    for b in range(B):
        block, reach, damping = blocks[b : b + 1], reaches[b : b + 1], damp_ref[b : b + 1, :]
        gap = jnp.maximum(jnp.maximum(first - block, block - last), 0.0)
        felt = (gap < reach).astype(F32)
        rank = dot(jnp.broadcast_to(felt, (8, K)).astype(BF16), upper)[0:1]
        chosen = jnp.where(felt > 0.0, rank - 1.0, -1.0) == slots
        most = jnp.maximum(most, jnp.sum(felt).astype(I32))
        pick_ref[b] = ones_where(chosen)
        cols_ref[b, 0] = jnp.broadcast_to(column(chosen, block), (K, LB))
        cols_ref[b, 1] = jnp.broadcast_to(jnp.maximum(column(chosen, reach), 1.0), (K, LB))
        cols_ref[b, 2] = jnp.broadcast_to(column(chosen, damping), (K, LB))
    count_ref[0] = sp_ref[0]
    count_ref[1] = sp_ref[1]
    count_ref[2] = most
    distance = jnp.abs(blocks[1:2] - column(diagonal, blocks[0:1]))
    reach = column(diagonal, reaches[0:1])
    damping = column(diagonal, damp_ref[0:1, :])
    w_ref[...] = damping * jnp.maximum(0.0, 1.0 - distance / reach)


def places(sp, segment, place, damping, extent):
    return pl.pallas_call(
        places_kernel,
        grid_spec=pltpu.PrefetchScalarGridSpec(
            num_scalar_prefetch=1,
            grid=(1,),
            in_specs=[whole((B, K))] * 4,
            out_specs=[
                whole((B, K, K)),
                whole((B, 3, K, LB)),
                whole((K, K)),
                pl.BlockSpec(memory_space=pltpu.SMEM),
            ],
        ),
        out_shape=[
            jax.ShapeDtypeStruct((B, K, K), BF16),
            jax.ShapeDtypeStruct((B, 3, K, LB), F32),
            jax.ShapeDtypeStruct((K, K), F32),
            jax.ShapeDtypeStruct((3,), I32),
        ],
        compiler_params=pltpu.CompilerParams(vmem_limit_bytes=VMEM_LIMIT),
        cost_estimate=pl.CostEstimate(
            flops=1_000_000, bytes_accessed=2_000_000, transcendentals=0
        ),
        name="places",
    )(sp, segment, place, damping, extent)


def observe_stats(prior, values, variances):
    centre = jnp.sum(prior, axis=0, keepdims=True) / MEMBERS
    anomaly = prior - centre
    prior_var = jnp.sum(anomaly * anomaly, axis=0, keepdims=True) / (MEMBERS - 1) + 1e-06
    post_var = 1.0 / (1.0 / prior_var + 1.0 / variances)
    post_mean = post_var * (centre / prior_var + values / variances)
    shrink = jnp.sqrt(post_var / prior_var)
    increment = (post_mean - centre + (shrink - 1.0) * anomaly).astype(BF16)
    scaled = (anomaly * (1.0 / ((MEMBERS - 1) * prior_var))).astype(BF16)
    left = jnp.sum(scaled.astype(F32), axis=0, keepdims=True) * (-1.0 / EXTRA)
    return increment, jnp.concatenate([scaled, jnp.broadcast_to(left, (EXTRA, K)).astype(BF16)], 0)


def with_extra(x):
    return jnp.concatenate([x, x[:EXTRA]], 0)


def stats_kernel(mine_ref, other_ref, val_ref, var_ref, pick_ref, w_ref, cov_ref, chg_ref):
    def prior(b):
        at = slice(b * K, (b + 1) * K)
        return jnp.concatenate([mine_ref[:, at].astype(F32), other_ref[:, at].astype(F32)], 0)

    increment0, scaled0 = observe_stats(prior(0), val_ref[0:1, :], var_ref[0:1, :])
    before = prior(1)
    eye = ones_where(iota((K, K), 0) == iota((K, K), 1))
    cov = dot(dot_nt(eye, scaled0).astype(BF16), with_extra(before.astype(BF16)))
    gain = (w_ref[...] * cov).astype(BF16)
    after = (before + dot(increment0, gain)).astype(BF16).astype(F32)
    increment1, scaled1 = observe_stats(after, val_ref[1:2, :], var_ref[1:2, :])
    for b, (increment, scaled) in enumerate(((increment0, scaled0), (increment1, scaled1))):
        cov_ref[b] = dot_nt(pick_ref[b], scaled).astype(BF16)
        chg_ref[b] = dot_nt(increment, pick_ref[b]).astype(BF16)


def stats(mine, other, readings, spread, picks, w):
    return pl.pallas_call(
        stats_kernel,
        grid=(1,),
        in_specs=[
            whole((HALF, B * K)),
            whole((HALF, B * K)),
            whole((B, K)),
            whole((B, K)),
            whole((B, K, K)),
            whole((K, K)),
        ],
        out_specs=[whole((B, K, DEPTH)), whole((B, MEMBERS, K))],
        out_shape=[
            jax.ShapeDtypeStruct((B, K, DEPTH), BF16),
            jax.ShapeDtypeStruct((B, MEMBERS, K), BF16),
        ],
        compiler_params=pltpu.CompilerParams(vmem_limit_bytes=VMEM_LIMIT),
        name="stats",
    )(mine, other, readings, spread, picks, w)


def moved(base, a):
    return pl.ds(pl.multiple_of(base + a, 256), 256)


def update_kernel(begin, sp_ref, cov_ref, chg_ref, cols, mine_ref, other_ref, *rest):
    own_ref, away_ref = rest[-2:]
    step = pl.program_id(0) + begin
    there = sp_ref[0] * SD + step * CHUNK
    back = pl.program_id(0) * CHUNK
    first = sp_ref[1].astype(F32)

    def weights(b, kc, start):
        block = (first + (step * CHUNK_BLOCKS + start).astype(F32)) + iota((kc, LB), 1).astype(F32)
        distance = jnp.abs(block - cols[b, 0, :kc])
        return cols[b, 2, :kc] * jnp.maximum(0.0, 1.0 - distance / cols[b, 1, :kc])

    def advance_pairs(kc, start):
        pairs = range(IN_FLIGHT[kc])
        at = [pl.multiple_of((start + p) * 256, 256) for p in pairs]
        w = [weights(b, kc, 2 * start) for b in range(B)]
        wide = [
            jnp.concatenate(
                [
                    mine_ref[:, pl.ds(a, 256)].astype(F32),
                    other_ref[:, moved(there, a)].astype(F32),
                ],
                0,
            )
            for a in at
        ]
        for b in range(B):
            cov = [dot(cov_ref[b, :kc], with_extra(x.astype(BF16))) for x in wide]
            gain = [
                jnp.concatenate(
                    [
                        c[:, h * LB : (h + 1) * LB]
                        * jnp.broadcast_to(w[b][:, 2 * p + h : 2 * p + h + 1], (kc, LB))
                        for h in range(2)
                    ],
                    1,
                ).astype(BF16)
                for p, c in zip(pairs, cov)
            ]
            wide = [x + dot(chg_ref[b, :, :kc], g) for x, g in zip(wide, gain)]
            if b == 0:
                wide = [x.astype(BF16).astype(F32) for x in wide]
        for a, x in zip(at, wide):
            own_ref[:, pl.ds(a, 256)] = x[:HALF].astype(BF16)
            away_ref[:, moved(back, a)] = x[HALF:].astype(BF16)

    def advance(kc):
        rounds = CHUNK // 256 // IN_FLIGHT[kc]

        def body(i, _):
            advance_pairs(kc, i * IN_FLIGHT[kc])
            return 0

        lax.fori_loop(0, rounds, body, 0)

    n = sp_ref[2]

    @pl.when(n <= 32)
    def _():
        advance(32)

    @pl.when((n > 32) & (n <= 64))
    def _():
        advance(64)

    @pl.when((n > 64) & (n <= 128))
    def _():
        advance(128)

    @pl.when(n > 128)
    def _():
        advance(K)


def update(begin, steps, info, cov, chg, cols, x, got, out):
    half = lambda i, s: (0, s[0] * STEPS + begin + i)
    in_specs = [pl.BlockSpec(memory_space=pltpu.VMEM)] * 3 + [
        pl.BlockSpec((HALF, CHUNK), half),
        pl.BlockSpec(memory_space=pltpu.VMEM),
    ]
    operands = [info, cov, chg, cols, x, got]
    aliases = {}
    if out is not None:
        in_specs.append(pl.BlockSpec(memory_space=pl.ANY))
        operands.append(out)
        aliases = {len(operands) - 1: 0}
    return pl.pallas_call(
        lambda *refs: update_kernel(begin, *refs),
        grid_spec=pltpu.PrefetchScalarGridSpec(
            num_scalar_prefetch=1,
            grid=(steps,),
            in_specs=in_specs,
            out_specs=[
                pl.BlockSpec((HALF, CHUNK), half),
                pl.BlockSpec(memory_space=pltpu.VMEM),
            ],
        ),
        out_shape=[
            jax.ShapeDtypeStruct((HALF, CHIP), BF16),
            jax.ShapeDtypeStruct((HALF, steps * CHUNK), BF16),
        ],
        input_output_aliases=aliases,
        compiler_params=pltpu.CompilerParams(vmem_limit_bytes=VMEM_LIMIT),
        cost_estimate=pl.CostEstimate(
            flops=600_000_000 * steps,
            bytes_accessed=4 * MEMBERS * CHUNK * steps,
            transcendentals=0,
        ),
        name=f"update{begin}",
    )(*operands)


def fill(begins, parts, out):
    def kernel(*refs):
        out_ref, sems = refs[-2:]
        base = (1 - lax.axis_index("mem")) * SD
        copies = []
        for j, (begin, part) in enumerate(zip(begins, refs[: len(parts)])):
            width = part.shape[1] // PIECES
            for p in range(PIECES):
                start = pl.multiple_of(base + begin * CHUNK + p * width, 1024)
                to = out_ref.at[:, pl.ds(start, width)]
                piece = part.at[:, pl.ds(p * width, width)]
                copies.append(pltpu.make_async_copy(piece, to, sems.at[j * PIECES + p]))
        for copy in copies:
            copy.start()
        for copy in copies:
            copy.wait()

    return pl.pallas_call(
        kernel,
        in_specs=[pl.BlockSpec(memory_space=pltpu.VMEM)] * len(parts)
        + [pl.BlockSpec(memory_space=pl.ANY)],
        out_specs=pl.BlockSpec(memory_space=pl.ANY),
        scratch_shapes=[pltpu.SemaphoreType.DMA((PIECES * len(parts),))],
        out_shape=jax.ShapeDtypeStruct((HALF, CHIP), BF16),
        input_output_aliases={len(parts): 0},
        compiler_params=pltpu.CompilerParams(vmem_limit_bytes=VMEM_LIMIT),
        name=f"fill{begins[0]}",
    )(*parts, out)


def sent(array, target):
    pairs = [(i, target(i)) for i in range(CHIPS)]
    return lax.ppermute(array, "state", [(i, j) for i, j in pairs if 0 <= j < CHIPS])


def along_row(array, bits):
    return sent(array, lambda i: i ^ bits)


def across_rows(array, first):
    def partner(i):
        row = i // 4
        return i + 4 if row % 2 == first else i - 4

    return sent(array, partner)


def swapped(array):
    return lax.ppermute(array, "mem", [(0, 1), (1, 0)])


def on_device(x, segment, place, readings, spread, damping, extent):
    core = lax.axis_index("mem")
    chip = lax.axis_index("state")
    sp = jnp.stack([core, (chip * 2 + core) * SEG_BLOCKS, chip]).astype(I32)

    picked = pick(sp, segment * SD + place, x)
    x, picked = lax.optimization_barrier((x, picked))
    two, one, three = (along_row(picked, bits) for bits in (2, 1, 3))
    got = swapped(x)
    picks, cols, w, info = places(sp, segment, place, damping, extent)
    near = picked + one + two + three
    near, picks, cols, w, info = lax.optimization_barrier((near, picks, cols, w, info))
    far = near + across_rows(near, 0) + across_rows(near, 1)
    cov, chg = stats(far, swapped(far), readings, spread, picks, w)
    out = None
    away = []
    begin = 0
    for steps in PARTS:
        out, part = update(begin, steps, info, cov, chg, cols, x, got, out)
        away.append((begin, swapped(part)))
        begin += steps
    for some in (away[:-1], away[-1:]):
        out = fill([begin for begin, _ in some], [part for _, part in some], out)
    return out


def solution(mesh):
    in_specs = (P("mem", "state"), P(), P(), P(), P(), P(), P())
    return jax.shard_map(
        on_device, mesh=mesh, in_specs=in_specs, out_specs=P("mem", "state"), check_vma=False
    )
```
